256 devices in a mesh: pipe: 4 (over y), expert: 64 (over z, x, core).
Axes of the slice: x: 4, y: 4, z: 8, core: 2. Of those that a mesh axis runs over, the one named last changes fastest.
Arguments:
- upstream: bfloat16 [4, 8192, 3584], P('pipe', 'expert'), may hold values from -6 to 6
- routes: int32 [4, 8192, 8], P('pipe', 'expert'), may hold values from 0 to 63, all different within a row; in each aligned block of 128 rows (0 to 127, 128 to 255, ..., all dimensions but the last counted through in order) at most 20 rows name the same one
- affinity: float32 [4, 8192, 8], P('pipe', 'expert'), may hold values from 0.02 to 0.98
- w_down: bfloat16 [4, 64, 1024, 3584], P('pipe', 'expert'), may hold values from -0.1875 to 0.1875
- saved_hidden: bfloat16 [4, 64, 1280, 1024], P('pipe', 'expert'), may hold values from -0.29882812 to 0.29882812
Outputs:
- hidden_grad: bfloat16 [4, 64, 1280, 1024], P('pipe', 'expert')
- affinity_grad: float32 [4, 8192, 8], P('pipe', 'expert')
The draws below stay inside these ranges and needn't reach their ends.
Inputs may be any that keep to these rules, and one draw needn't show every extreme that they name: `routes`: each token names 8 different experts. Within one device's block of 128 tokens of a section no expert is named by more than 20 tokens, and in some block one expert is named by exactly 20.
All inputs are finite; a program needn't handle non-finite values.
Results may differ from the reference program's by a relative error of at most 0.0049.
Values may be sent and summed in bfloat16 or wider, within the bound.
No kernel may reach another device: no remote copies, remote signals or barrier semaphores. Data moves between devices by JAX's collectives and lax.ppermute only.
A program may use at most 128 MiB of HBM per device.

```python
import math
from functools import partial
import jax
import jax.numpy as jnp
import numpy as np
from jax import lax

D = 3584
H = 1024
TOP = 8
TOK_DEV = 128
SECTIONS = 4
EXPERTS = 64
TOKENS = 8192
MOST = 20
SLOTS = 1280
N_EXPERT = 64


def shard_levels(rng, extent, shards, smallest, high):
    loudness, own = 1.0, jax.random.fold_in(rng, 6)
    for dim, shards_of in shards:
        steps = jnp.exp(jax.random.uniform(jax.random.fold_in(own, dim), (shards_of,), jnp.float32, smallest / len(shards), high / len(shards)))
        loudness = loudness * jnp.repeat(steps, extent[dim] // shards_of).reshape([-1 if axis == dim else 1 for axis in range(len(extent))])
    return loudness


def deal_out(key, own, number, rows, count, top, most, skew):
    ranking = jax.random.permutation(key, count)
    crowded, common = load_shares(count, rows * top, most, skew, True), load_shares(count, rows * top, most, skew, False)
    places = jnp.arange(count)

    def named(sizes, turn):
        used = int((sizes > 0).sum())
        fixed = max(1, used // 4)
        moved = fixed + (places - fixed + turn * (used - fixed)) % max(1, count - fixed)
        return jnp.zeros((count,), jnp.int32).at[ranking[jnp.where(places < fixed, places, moved)]].set(jnp.asarray(sizes, jnp.int32))

    sizes = jnp.where(number % 4 == 0, named(crowded, number // 4), named(common, number - number // 4 - 1))
    mixed = jax.random.permutation(jax.random.fold_in(own, 3), count)
    giver, sink = mixed[0:count // 2 * 2:2], mixed[1:count // 2 * 2:2]
    margin = jnp.minimum(sizes[giver] - 1, most - sizes[sink]) // 2
    margin = jnp.where((giver == ranking[0]) | (sink == ranking[0]) | (sizes[sink] == 0), 0, jnp.maximum(margin, 0))
    moved = jax.random.randint(jax.random.fold_in(own, 4), (count // 2,), 0, 1 << 20) % (margin + 1)
    sizes = sizes.at[giver].add(-moved).at[sink].add(moved)
    members = jnp.searchsorted(jnp.cumsum(sizes), jnp.arange(rows * top), side="right").astype(jnp.int32)
    grid = members.reshape(top, rows).T
    grid = grid[jax.random.permutation(jax.random.fold_in(own, 1), rows)]
    turn = jax.random.randint(jax.random.fold_in(own, 2), (rows, 1), 0, top)
    return jnp.take_along_axis(grid, (jnp.arange(top)[None, :] + turn) % top, axis=1)


def load_shares(number_of, total, limit, skew, full):
    weights = [(1 << 20) // math.isqrt(rank ** skew) + 1 for rank in range(1, number_of + 1)]
    largest = limit if full else min(limit, max(-(-total // number_of), total * weights[0] // sum(weights)))
    least = 1 if total - largest >= number_of - 1 else 0
    holding, spare = [largest] + [least] * (number_of - 1), total - largest - least * (number_of - 1)
    while spare > 0:
        free = [i for i in range(1, number_of) if holding[i] < largest] or [i for i in range(1, number_of) if holding[i] < limit]
        pool, budget = sum([weights[i] for i in free]), spare
        for i in free:
            extra = min(limit - holding[i], max(1, budget * weights[i] // pool), spare)
            holding[i] = holding[i] + extra
            spare = spare - extra
    return np.array(holding)


def noise(stream_key, shape, deviation, reach, pieces=(), kind=jnp.bfloat16):
    drawn = jax.random.normal(stream_key, shape, jnp.float32) * deviation
    if len(pieces) > 0:
        drawn = shard_levels(stream_key, shape, pieces, -0.22, 0.18) * drawn
    return jnp.clip(drawn, min=-reach, max=reach).astype(kind)


def setup_inputs(seed: int = 0) -> dict:
    keys = jax.random.split(jax.random.key(seed), 6)
    upstream = noise(keys[0], (SECTIONS, TOKENS, D), 1.0, 6.0, ((0, 4), (1, 64)))
    routes_keys = jax.random.split(jax.random.fold_in(keys[1], 1), SECTIONS * TOKENS // TOK_DEV)
    routes_turns = jax.random.permutation(jax.random.fold_in(keys[1], 3), SECTIONS * TOKENS // TOK_DEV)
    routes = jax.vmap(lambda own, number: deal_out(jax.random.fold_in(keys[1], 2), own, number, TOK_DEV, EXPERTS, TOP, MOST, 1))(routes_keys, routes_turns).reshape((SECTIONS, TOKENS, TOP))
    affinity = jnp.clip(jnp.exp(math.log(0.98) - 3.89182034 * jax.random.uniform(keys[2], (SECTIONS, TOKENS, TOP), jnp.float32) ** shard_levels(keys[2], (SECTIONS, TOKENS, TOP), ((0, 4), (1, 64)), -0.2, 0.2)), 0.02, 0.98)
    w_down = noise(keys[3], (SECTIONS, EXPERTS, H, D), H ** -0.5, 0.1875, ((0, 4), (1, 64)))
    saved_hidden = noise(keys[4], (SECTIONS, EXPERTS, SLOTS, H), 0.05, 0.29882812, ((0, 4), (1, 64)))
    return {"upstream": upstream, "routes": routes, "affinity": affinity, "w_down": w_down, "saved_hidden": saved_hidden}


SCALE_ROUTED = 2.5


def rank_slots(token_routes, experts_count):
    labels = jnp.arange(experts_count, dtype=jnp.int32)
    onehot = jnp.sum((token_routes[:, :, None] == labels).astype(jnp.int32), axis=1).astype(jnp.int32)
    before = (jnp.cumsum(onehot, axis=0) - onehot).astype(jnp.int32)
    return jnp.take_along_axis(before, token_routes, axis=1).astype(jnp.int32)


def section_grads(incoming, token_routes, weights_raw, weight_stack, saved_stack):
    totals = jnp.sum(weights_raw, axis=1)
    gate_weights = (SCALE_ROUTED * weights_raw / totals[:, None]).astype(jnp.bfloat16)
    blocks = token_routes.reshape(N_EXPERT, TOK_DEV, TOP)
    rank_list = jax.vmap(partial(rank_slots, experts_count=EXPERTS))(blocks).reshape(TOKENS, TOP)
    block_base = ((jnp.arange(TOKENS, dtype=jnp.int32) // TOK_DEV) * MOST).astype(jnp.int32)[:, None]
    slot_index = (block_base + rank_list).astype(jnp.int32)

    def per_expert(operands):
        expert_id, weight_one, saved_one = operands
        matches = token_routes == expert_id
        is_taken = jnp.any(matches, axis=1)
        chosen = jnp.sum(jnp.where(matches, slot_index, 0), axis=1).astype(jnp.int32)
        target = jnp.where(is_taken, chosen, SLOTS).astype(jnp.int32)
        dispatched = jnp.zeros((SLOTS, D), jnp.bfloat16).at[target].set(incoming, mode="drop")
        chosen_gain = jnp.sum(jnp.where(matches, gate_weights.astype(jnp.float32), jnp.float32(0.0)), axis=1)
        slot_gains = jnp.zeros((SLOTS,), jnp.float32).at[target].set(chosen_gain, mode="drop")
        projected = jnp.dot(dispatched, weight_one.T, preferred_element_type=jnp.float32)
        hidden_grad = (slot_gains[:, None] * projected).astype(jnp.bfloat16)
        slot_scores = jnp.sum(projected * saved_one.astype(jnp.float32), axis=1)
        return hidden_grad, slot_scores

    hidden_all, scores_all = lax.map(per_expert, (jnp.arange(EXPERTS, dtype=jnp.int32), weight_stack, saved_stack))
    gate_grad = scores_all[token_routes, slot_index]
    weighted_sum = jnp.sum(gate_weights.astype(jnp.float32) * gate_grad, axis=1)
    affinity_grad = (SCALE_ROUTED / totals)[:, None] * gate_grad - (weighted_sum / totals)[:, None]
    return hidden_all, affinity_grad


def reference(upstream, routes, affinity, w_down, saved_hidden):
    hidden_list = []
    affinity_list = []
    for section in range(SECTIONS):
        source_section = min(section + 1, SECTIONS - 1)
        hidden_all, affinity_grad = section_grads(upstream[source_section], routes[section], affinity[section], w_down[section], saved_hidden[section])
        hidden_list.append(hidden_all)
        affinity_list.append(affinity_grad)
    return jnp.stack(hidden_list), jnp.stack(affinity_list)
```

```python
from functools import partial

import jax
import jax.numpy as jnp
from jax import lax
from jax.experimental import pallas as pl
from jax.experimental.pallas import tpu as pltpu
from jax.sharding import Mesh, PartitionSpec as P

SCALE_ROUTED = 2.5
CORES = 2
COLUMNS = 4
LANES = 128
VMEM_BYTES = 48 * 2**20


def iota(shape, dim):
    return lax.broadcasted_iota(jnp.int32, shape, dim)


def call(body, out_shape, cost, **kwargs):
    return pl.pallas_call(
        body,
        out_shape=out_shape,
        cost_estimate=pl.CostEstimate(flops=cost[0], bytes_accessed=cost[1], transcendentals=0),
        compiler_params=pltpu.CompilerParams(vmem_limit_bytes=VMEM_BYTES),
        **kwargs,
    )


def ranks_before(hits):
    tokens = hits.shape[1]
    first, second = iota((tokens, tokens), 0), iota((tokens, tokens), 1)
    ahead = (first < second) & (first // LANES == second // LANES)
    ahead = jnp.where(ahead, 1.0, 0.0).astype(jnp.bfloat16)
    return jnp.dot(hits.astype(jnp.bfloat16), ahead, preferred_element_type=jnp.float32)


def gate_rows(affinity):
    total = jnp.sum(affinity, axis=0, keepdims=True)
    weights = (SCALE_ROUTED * affinity / total).astype(jnp.bfloat16).astype(jnp.float32)
    return total, weights


def routing_kernel(capacity, routes_ref, affinity_ref, gains_ref, slot_ref):
    experts = slot_ref.shape[0]
    _, weights = gate_rows(affinity_ref[...])
    labels = iota((experts, LANES), 0)
    hits = jnp.zeros((experts, LANES), jnp.float32)
    gains = jnp.zeros((experts, LANES), jnp.float32)
    for k in range(routes_ref.shape[0]):
        same = routes_ref[k : k + 1, :] == labels
        hits += jnp.where(same, 1.0, 0.0)
        gains += jnp.where(same, weights[k : k + 1, :], 0.0)
    slot = jnp.where(hits > 0, ranks_before(hits), -1.0).astype(jnp.int32)
    slot_ref[...] = slot
    lane = iota((experts, LANES), 1)
    table = jnp.zeros((experts, LANES), jnp.float32)
    for r in range(capacity):
        column = jnp.sum(jnp.where(slot == r, gains, 0.0), axis=1, keepdims=True)
        table = jnp.where(lane == r, column, table)
    gains_ref[...] = table


def select_kernel(parts, capacity, place_ref, *refs):
    routes = refs[: max(parts) + 1]
    blocks = refs[len(routes) : len(routes) + len(parts)]
    out_ref, onehot_ref = refs[-2:]
    rows, tokens = onehot_ref.shape[1:]
    experts = rows // (CORES * capacity)
    part = pl.program_id(0)

    @pl.when((part == 0) & (pl.program_id(1) == 0))
    def _():
        for i, routes_ref in enumerate(routes):
            labels = place_ref[0] * experts + iota((16, tokens), 0)
            hits = jnp.zeros((16, tokens), jnp.float32)
            for k in range(routes_ref.shape[0]):
                hits += jnp.where(routes_ref[k : k + 1, :] == labels, 1.0, 0.0)
            slot = ranks_before(hits).astype(jnp.int32) + (iota((16, tokens), 1) // LANES) * capacity
            slot = jnp.where(hits > 0, slot, -1)
            each = CORES * capacity
            order = iota((each, tokens), 0)
            for s in range(experts):
                mine = jnp.where(order == slot[s : s + 1, :], 1.0, 0.0)
                onehot_ref[i, s * each : (s + 1) * each, :] = mine

    for j, block_ref in enumerate(blocks):

        @pl.when(part == j)
        def _(j=j, block_ref=block_ref):
            out_ref[...] = jnp.dot(
                onehot_ref[parts[j]].astype(jnp.bfloat16),
                block_ref[...],
                preferred_element_type=jnp.float32,
            ).astype(jnp.bfloat16)


def select_rows(place, routes, blocks, parts, experts, capacity):
    tokens, width = blocks[0].shape
    rows = experts * CORES * capacity
    tile = width // 2
    count = len(blocks)

    def held(j):
        def index(h, n, place):
            return 0, jnp.where(h == j, n, jnp.where(h < j, 0, 1))

        return index

    def target(h, n, place):
        if count == 1:
            return 0, n
        return 0, jnp.where(h < 2, jnp.bitwise_xor(h, place[1]), h) * 2 + n

    whole = [pl.BlockSpec(r.shape, lambda h, n, place: (0, 0)) for r in routes]
    return call(
        partial(select_kernel, parts, capacity),
        jax.ShapeDtypeStruct((rows, width * count), jnp.bfloat16),
        (2 * rows * tokens * width * count, 2 * (rows + tokens) * width * count),
        grid_spec=pltpu.PrefetchScalarGridSpec(
            num_scalar_prefetch=1,
            grid=(count, 2),
            in_specs=whole + [pl.BlockSpec((tokens, tile), held(j)) for j in range(count)],
            out_specs=pl.BlockSpec((rows, tile), target),
            scratch_shapes=[pltpu.VMEM((len(routes), rows, tokens), jnp.float32)],
        ),
    )(place, *routes, *blocks)


def project_kernel(full, half, capacity, zs_ref, x_ref, w_ref, saved_ref, gains_ref, scores_in, *refs):
    hidden_ref, scores_ref, acc_ref, gain_ref, part_ref = refs[-5:]
    n, j = pl.program_id(0), pl.program_id(1)
    slots, width = acc_ref.shape[1:]
    each = CORES * capacity
    features = w_ref.shape[1]
    middle = features // 2
    dims = (((1,), (1,)), ((), ()))

    def times(x, w):
        return lax.dot_general(x, w, dims, preferred_element_type=jnp.float32)

    @pl.when(j == 0)
    def _():
        at = 0
        if full:
            y = times(x_ref[:, :features], w_ref[...])
            for c in range(CORES):
                for x in range(COLUMNS):
                    top = (x * CORES + c) * each
                    acc_ref[c, x * each : (x + 1) * each, :] = y[top : top + each]
            at = features
        if half:
            low = times(x_ref[:, at : at + middle], w_ref[:, :middle])
            high = times(x_ref[:, at : at + middle], w_ref[:, middle:])
            for x in range(COLUMNS):
                top = x * CORES * each
                acc_ref[CORES * full, x * each : (x + 1) * each, :] = (
                    low[top : top + each] + high[top + each : top + 2 * each]
                )

    @pl.when((n == 0) & (j == 0))
    def _():
        scores_ref[...] = scores_in[...]

    row = iota((slots, LANES), 0)
    lane = iota((slots, LANES), 1)
    sources = slots // capacity
    first = pl.multiple_of(zs_ref[j] * sources, sources)
    own_lane = lane == row % capacity

    @pl.when(n == 0)
    def _():
        table = gains_ref[pl.ds(first, sources), :]
        spread = jnp.zeros((slots, LANES), jnp.float32)
        for s in range(sources):
            spread = jnp.where(row // capacity == s, table[s : s + 1, :], spread)
        column = jnp.sum(jnp.where(own_lane, spread, 0.0), axis=1, keepdims=True)
        gain_ref[j] = jnp.broadcast_to(column, (slots, LANES))
        part_ref[j] = jnp.zeros((slots, LANES), jnp.float32)

    gain = gain_ref[j]
    total = part_ref[j]
    for i in range(width // LANES):
        lanes = slice(i * LANES, (i + 1) * LANES)
        projected = acc_ref[j, :, lanes]
        hidden_ref[0, :, lanes] = (gain * projected).astype(jnp.bfloat16)
        total += projected * saved_ref[0, :, lanes].astype(jnp.float32)
    part_ref[j] = total

    @pl.when(n == pl.num_programs(0) - 1)
    def _():
        column = jnp.sum(total, axis=1, keepdims=True)
        spread = jnp.where(own_lane, column, 0.0)
        place = iota((sources, LANES), 0)
        table = jnp.zeros((sources, LANES), jnp.float32)
        for s in range(sources):
            line = jnp.sum(jnp.where(row // capacity == s, spread, 0.0), axis=0, keepdims=True)
            table = jnp.where(place == s, line, table)
        scores_ref[pl.ds(first, sources), :] = table


def project(zs, rows, weight, saved, gains, scores, hidden, full, half, capacity):
    count = CORES * full + half
    blocks, slots, units = saved.shape
    features = weight.shape[1]
    width = 256
    constant = lambda n, j, zs: (0, 0)
    by_block = lambda n, j, zs: (zs[j], 0, n)
    in_specs = [
        pl.BlockSpec(rows.shape, constant),
        pl.BlockSpec((width, features), lambda n, j, zs: (n, 0)),
        pl.BlockSpec((1, slots, width), by_block),
        pl.BlockSpec(gains.shape, constant),
        pl.BlockSpec(scores.shape, constant),
    ]
    operands = [zs, rows, weight, saved, gains, scores]
    aliases = {}
    if hidden is not None:
        in_specs.append(pl.BlockSpec(memory_space=pl.ANY))
        aliases = {len(operands): 0}
        operands.append(hidden)
    return call(
        partial(project_kernel, full, half, capacity),
        (
            jax.ShapeDtypeStruct(saved.shape, jnp.bfloat16),
            jax.ShapeDtypeStruct(scores.shape, jnp.float32),
        ),
        (2 * rows.size * units, 2 * (rows.size + weight.size + 2 * count * slots * units)),
        grid_spec=pltpu.PrefetchScalarGridSpec(
            num_scalar_prefetch=1,
            grid=(units // width, count),
            in_specs=in_specs,
            out_specs=(pl.BlockSpec((1, slots, width), by_block), pl.BlockSpec(scores.shape, constant)),
            scratch_shapes=[
                pltpu.VMEM((count, slots, width), jnp.float32),
                pltpu.VMEM((count, slots, LANES), jnp.float32),
                pltpu.VMEM((count, slots, LANES), jnp.float32),
            ],
        ),
        input_output_aliases=aliases,
    )(*operands)


def gate_kernel(capacity, scores_ref, slot_ref, routes_ref, affinity_ref, out_ref):
    top = routes_ref.shape[0]
    total, weights = gate_rows(affinity_ref[...])
    slot = slot_ref[...]
    found = jnp.zeros(slot.shape, jnp.float32)
    for r in range(capacity):
        found = jnp.where(slot == r, scores_ref[:, r : r + 1], found)
    labels = iota(slot.shape, 0)
    place = iota((top, LANES), 0)
    grad = jnp.zeros((top, LANES), jnp.float32)
    for k in range(top):
        line = jnp.sum(jnp.where(routes_ref[k : k + 1, :] == labels, found, 0.0), axis=0, keepdims=True)
        grad = jnp.where(place == k, line, grad)
    weighted = jnp.sum(weights * grad, axis=0, keepdims=True)
    out_ref[...] = (SCALE_ROUTED / total) * grad - weighted / total


def on_device(upstream, routes, affinity, w_down, saved_hidden):
    sections, depth = lax.axis_size("pipe"), lax.axis_size("z")
    section, z, core = lax.axis_index("pipe"), lax.axis_index("z"), lax.axis_index("core")
    everyone = ("z", "x", "core")
    expert_count = depth * COLUMNS * CORES
    local = COLUMNS * CORES
    slot_total, units = saved_hidden.shape[2:]
    capacity = slot_total // expert_count
    tokens, features = upstream.shape[1:]
    half = features // 2
    cores = range(CORES)

    mine = lax.dynamic_slice(upstream[0], (0, core * half), (tokens, half))
    other = lax.dynamic_slice(upstream[0], (0, (1 - core) * half), (tokens, half))
    hop = range(1, sections)
    last = sections - 1
    near = lax.ppermute(mine, ("pipe", "core"), [(i * CORES + c, (i - 1) * CORES + c) for i in hop for c in cores])
    far = lax.ppermute(other, ("pipe", "core"), [(i * CORES + c, (i - 1) * CORES + 1 - c) for i in hop for c in cores])
    stay = lax.ppermute(other, ("pipe", "core"), [(last * CORES + c, last * CORES + 1 - c) for c in cores])

    routes_own = routes[0].T
    affinity_own = affinity[0].T
    routes_mate = lax.ppermute(routes_own, "core", [(c, 1 - c) for c in cores])

    def in_order(a, b, axis):
        return jnp.where(core == 0, jnp.concatenate([a, b], axis), jnp.concatenate([b, a], axis))

    def along(block, distance, cross=False):
        pairs = []
        for i in range(depth):
            pairs.append((i * CORES + (1 if cross else 0), (i + distance) % depth * CORES))
            pairs.append((i * CORES + (0 if cross else 1), (i - distance) % depth * CORES + 1))
        return lax.ppermute(block, ("z", "core"), pairs)

    reach = depth // 2
    routes_at = [in_order(routes_own, routes_mate, 1)]
    routes_at += [along(routes_at[0], k) for k in range(1, reach + 1)]

    gains, slot_of = call(
        partial(routing_kernel, capacity),
        (
            jax.ShapeDtypeStruct((expert_count, LANES), jnp.float32),
            jax.ShapeDtypeStruct((expert_count, LANES), jnp.int32),
        ),
        (10**6, 10**5),
    )(routes_own, affinity_own)

    def exchange(block, axes, parts):
        shape = block.shape
        block = block.reshape(parts, shape[0] // parts, shape[1])
        return lax.all_to_all(block, axes, split_axis=0, concat_axis=0, tiled=True).reshape(shape)

    gains = exchange(gains, everyone, expert_count)

    is_last = section == last
    held = in_order(jnp.where(is_last, mine, near), jnp.where(is_last, stay, far), 0)
    same, cross = [along(held, 1)], [along(held, 1, cross=True)]
    for k in range(1, reach):
        same.append(along(same[-1], 1))
        if k < reach - 1:
            cross.append(along(cross[-1], 1))

    place = jnp.stack([z, core])

    def columns(group_routes, blocks, parts):
        rows = select_rows(place, group_routes, blocks, parts, local, capacity)
        return exchange(rows, ("x", "core"), local)

    def at(*distances):
        return jnp.stack([(z + d) % depth for d in distances])

    weight = w_down[0, 0]
    saved = saved_hidden[0, 0].reshape(depth, slot_total // depth, units)
    scores = jnp.zeros((expert_count, LANES), jnp.float32)

    got = columns(routes_at[:1], [held], (0,))
    hidden, scores = project(at(0), got, weight, saved, gains, scores, None, 0, 1, capacity)
    for k in range(1, reach - 1):
        got = columns([routes_at[k]], [same[k - 1], cross[k - 1]], (0, 0))
        hidden, scores = project(at(-k, k), got, weight, saved, gains, scores, hidden, 1, 0, capacity)
    k = reach - 1
    got = columns(routes_at[k:], [same[k - 1], cross[k - 1], same[k]], (0, 0, 1))
    hidden, scores = project(at(-k, k, reach), got, weight, saved, gains, scores, hidden, 1, 1, capacity)

    returned = exchange(scores, everyone, expert_count)
    affinity_grad = call(
        partial(gate_kernel, capacity),
        jax.ShapeDtypeStruct(affinity_own.shape, jnp.float32),
        (10**6, 10**5),
    )(returned, slot_of, routes_own, affinity_own)
    return hidden.reshape(1, 1, slot_total, units), affinity_grad.T[None]


def solution(mesh):
    sections, experts = mesh.devices.shape
    grid = mesh.devices.reshape(sections, experts // (COLUMNS * CORES), COLUMNS, CORES)
    rows = ("z", "x", "core")
    return jax.shard_map(
        on_device,
        mesh=Mesh(grid, ("pipe",) + rows),
        in_specs=(
            P("pipe", rows, None),
            P("pipe", rows, None),
            P("pipe", rows, None),
            P("pipe", rows, None, None),
            P("pipe", rows, None, None),
        ),
        out_specs=(P("pipe", rows, None, None), P("pipe", rows, None)),
        check_vma=False,
    )
```

```python
from functools import partial

import jax
import jax.numpy as jnp
from jax import lax
from jax.experimental import pallas as pl
from jax.experimental.pallas import tpu as pltpu
from jax.sharding import Mesh, PartitionSpec as P

SCALE_ROUTED = 2.5
CORES = 2
COSTS = 3.0, 3.0, 14.0, 8.0
COLUMNS = 4
LANES = 128
SMALL_VMEM = 60 * 2**20
PROJECT_VMEM = 57 * 2**20


def iota(shape, dim):
    return lax.broadcasted_iota(jnp.int32, shape, dim)


def call(body, out_shape, cost, vmem=SMALL_VMEM, **kwargs):
    return pl.pallas_call(
        body,
        out_shape=out_shape,
        cost_estimate=pl.CostEstimate(flops=cost[0], bytes_accessed=cost[1], transcendentals=0),
        compiler_params=pltpu.CompilerParams(vmem_limit_bytes=vmem),
        **kwargs,
    )


def ranks_before(hits):
    tokens = hits.shape[1]
    first, second = iota((tokens, tokens), 0), iota((tokens, tokens), 1)
    ahead = (first < second) & (first // LANES == second // LANES)
    ahead = jnp.where(ahead, 1.0, 0.0).astype(jnp.bfloat16)
    return jnp.dot(hits.astype(jnp.bfloat16), ahead, preferred_element_type=jnp.float32)


def gate_rows(affinity):
    total = jnp.sum(affinity, axis=0, keepdims=True)
    weights = (SCALE_ROUTED * affinity / total).astype(jnp.bfloat16).astype(jnp.float32)
    return total, weights


def match_kernel(capacity, place_ref, *refs):
    groups = refs[:-3]
    onehot_ref, gain_ref, token_ref = refs[-3:]
    rows, tokens = onehot_ref.shape[1:]
    each = CORES * capacity
    experts = rows // each
    token_ref[...] = jnp.zeros(token_ref.shape, jnp.float32)
    lane = iota((each, LANES), 1)
    last = gain_ref.shape[0] - 1
    for i, group_ref in enumerate(groups):
        top = group_ref.shape[0] // 2
        _, weights = gate_rows(group_ref[top:])
        labels = (place_ref[0] * experts + iota((16, tokens), 0)).astype(jnp.float32)
        hits = jnp.zeros((16, tokens), jnp.float32)
        gains = jnp.zeros((16, tokens), jnp.float32)
        for k in range(top):
            named = group_ref[k : k + 1, :] == labels
            hits += jnp.where(named, 1.0, 0.0)
            gains += jnp.where(named, weights[k : k + 1, :], 0.0)
        slot = ranks_before(hits).astype(jnp.int32) + (iota((16, tokens), 1) // LANES) * capacity
        slot = jnp.where(hits > 0, slot, -1)
        order = iota((each, tokens), 0)
        for at in range(experts):
            s = (at % COLUMNS) * CORES + at // COLUMNS
            found = order == slot[s : s + 1, :]
            here = slice(at * each, (at + 1) * each)
            onehot_ref[i, here] = jnp.where(found, 1.0, 0.0)
            column = jnp.sum(jnp.where(found, gains[s : s + 1, :], 0.0), axis=1, keepdims=True)
            if i <= last:
                gain_ref[i, here] = jnp.where(lane == 0, column, 0.0)
            else:
                gain_ref[last, here] += jnp.where(lane == 1, column, 0.0)


def select_kernel(parts, place_ref, onehot_hbm, gain_hbm, token_ref, *refs):
    blocks = refs[: len(parts)]
    out_hbm, token_out, onehot_ref, gain_in, gain_ref, in_ref, out_ref, sems, in_sems, out_sems = refs[len(parts) :]
    count, tokens, width = in_ref.shape
    tile = width // 2
    token_out[...] = token_ref[...]
    first = parts[0]
    tables = [
        pltpu.make_async_copy(onehot_hbm.at[pl.ds(first, onehot_ref.shape[0])], onehot_ref, sems.at[0]),
        pltpu.make_async_copy(gain_hbm.at[first], gain_in, sems.at[1]),
    ]
    loads, targets = [], []
    for j in range(count):
        half = j if count == 1 or j == 2 else jnp.bitwise_xor(j, place_ref[1])
        for h in range(2):
            lanes = slice(h * tile, (h + 1) * tile)
            loads.append(pltpu.make_async_copy(blocks[j].at[:, lanes], in_ref.at[j, :, lanes], in_sems.at[len(loads)]))
            at = pl.multiple_of(half * width + h * tile, LANES)
            targets.append(out_hbm.at[:, pl.ds(at, tile)])
    for load in tables[:1] + loads + tables[1:]:
        load.start()
    tables[0].wait()
    onehots = [onehot_ref[i].astype(jnp.bfloat16) for i in range(onehot_ref.shape[0])]
    stores = []
    for i, load in enumerate(loads):
        j, lanes = i // 2, slice(i % 2 * tile, (i % 2 + 1) * tile)
        load.wait()
        rows = jnp.dot(onehots[parts[j] - first], in_ref[j, :, lanes], preferred_element_type=jnp.float32)
        out_ref[j, :, lanes] = rows.astype(jnp.bfloat16)
        stores.append(pltpu.make_async_copy(out_ref.at[j, :, lanes], targets[i], out_sems.at[i]))
        stores[-1].start()
    tables[1].wait()
    gain_ref[...] = gain_in[...].astype(jnp.bfloat16)
    stores.append(pltpu.make_async_copy(gain_ref, out_hbm.at[:, count * width :], out_sems.at[len(loads)]))
    stores[-1].start()
    for store in stores:
        store.wait()


def select_rows(place, onehots, gains, token, blocks, parts, micros):
    tokens, width = blocks[0].shape
    rows = onehots.shape[1]
    count = len(blocks)
    groups = max(parts) - parts[0] + 1
    outside = pl.BlockSpec(memory_space=pltpu.HBM)
    inside = pl.BlockSpec(memory_space=pltpu.VMEM)
    return call(
        partial(select_kernel, parts),
        (
            jax.ShapeDtypeStruct((rows, width * count + LANES), jnp.bfloat16),
            jax.ShapeDtypeStruct(token.shape, token.dtype),
        ),
        (int(micros * 1.1e9), 2 * (rows + tokens) * width * count),
        grid_spec=pltpu.PrefetchScalarGridSpec(
            num_scalar_prefetch=1,
            in_specs=[outside, outside, inside] + [outside] * count,
            out_specs=(outside, inside),
            scratch_shapes=[
                pltpu.VMEM((groups, rows, tokens), jnp.float32),
                pltpu.VMEM((rows, LANES), jnp.float32),
                pltpu.VMEM((rows, LANES), jnp.bfloat16),
                pltpu.VMEM((count, tokens, width), jnp.bfloat16),
                pltpu.VMEM((count, rows, width), jnp.bfloat16),
                pltpu.SemaphoreType.DMA((2,)),
                pltpu.SemaphoreType.DMA((2 * count,)),
                pltpu.SemaphoreType.DMA((2 * count + 1,)),
            ],
        ),
    )(place, onehots, gains, token, *blocks)


def project_kernel(full, half, capacity, zs_ref, x_hbm, w_hbm, saved_hbm, scores_in, *refs):
    hidden_hbm, scores_ref = refs[-12:-10]
    x_ref, gain_ref, w_ref, saved_ref, y_ref, out_ref, x_sems, w_sems, saved_sems, out_sems = refs[-10:]
    blocks, slots, units = out_ref.shape
    middle = x_ref.shape[2]
    width = y_ref.shape[1]
    chunks = units // width
    dims = (((1,), (1,)), ((), ()))
    pieces = []
    if full:
        for c in range(2):
            pieces.append((x_hbm.at[:, c * middle : (c + 1) * middle], x_ref.at[c, : 2 * slots]))
    if half:
        at = 2 * middle * full
        for c in range(2):
            pieces.append(
                (x_hbm.at[c * slots : (c + 1) * slots, at : at + middle], x_ref.at[c, 2 * slots * full :])
            )
    at = middle * (2 * full + half)
    pieces.append((x_hbm.at[:, at : at + LANES], gain_ref))
    loads = [pltpu.make_async_copy(a, b, x_sems.at[i]) for i, (a, b) in enumerate(pieces)]
    w_loads = [
        pltpu.make_async_copy(
            w_hbm.at[n * width : (n + 1) * width], w_ref.at[n * width : (n + 1) * width], w_sems.at[n]
        )
        for n in range(chunks)
    ]
    saved_loads = [
        pltpu.make_async_copy(saved_hbm.at[zs_ref[j]], saved_ref.at[j], saved_sems.at[j]) for j in range(blocks)
    ]
    for load in loads + w_loads[:1] + saved_loads + w_loads[1:]:
        load.start()

    def times(x, w):
        return lax.dot_general(x, w, dims, preferred_element_type=jnp.float32)

    row = iota((slots, LANES), 0)
    own_lane = iota((slots, LANES), 1) == row % capacity
    sources = slots // capacity
    scores_ref[...] = scores_in[...]
    for load in loads:
        load.wait()
    gains, totals = [], []
    for j in range(blocks):
        whole = full and j < CORES
        top = j * slots if whole else 0
        lane = 0 if whole or not full else 1
        column = gain_ref[top : top + slots, lane : lane + 1].astype(jnp.float32)
        gains.append(jnp.broadcast_to(column, (slots, LANES)))
        totals.append(jnp.zeros((slots, LANES), jnp.float32))

    stores = []
    for n in range(chunks):
        here = slice(n * width, (n + 1) * width)
        w_loads[n].wait()
        y_ref[...] = times(x_ref[0], w_ref[here, :middle]) + times(x_ref[1], w_ref[here, middle:])
        for j in range(blocks):
            if n == 0:
                saved_loads[j].wait()
            for i in range(0, width, LANES):
                lanes = slice(n * width + i, n * width + i + LANES)
                projected = y_ref[j * slots : (j + 1) * slots, i : i + LANES]
                out_ref[j, :, lanes] = (gains[j] * projected).astype(jnp.bfloat16)
                totals[j] += projected * saved_ref[j, :, lanes].astype(jnp.float32)
            store = pltpu.make_async_copy(
                out_ref.at[j, :, here], hidden_hbm.at[zs_ref[j], :, here], out_sems.at[n * blocks + j]
            )
            store.start()
            stores.append(store)

    for j in range(blocks):
        column = jnp.sum(totals[j], axis=1, keepdims=True)
        spread = jnp.where(own_lane, column, 0.0)
        place = iota((sources, LANES), 0)
        table = jnp.zeros((sources, LANES), jnp.float32)
        for s in range(sources):
            line = jnp.sum(jnp.where(row // capacity == s, spread, 0.0), axis=0, keepdims=True)
            table = jnp.where(place == s, line, table)
        scores_ref[pl.ds(pl.multiple_of(zs_ref[j] * sources, sources), sources), :] = table
    for store in stores:
        store.wait()


def project(zs, rows, weight, saved, scores, hidden, full, half, capacity):
    count = CORES * full + half
    blocks, slots, units = saved.shape
    features = weight.shape[1]
    width = 256
    inside = pl.BlockSpec(memory_space=pltpu.VMEM)
    outside = pl.BlockSpec(memory_space=pltpu.HBM)
    in_specs = [outside] * 3 + [inside]
    operands = [zs, rows, weight, saved, scores]
    aliases = {}
    if hidden is not None:
        in_specs.append(outside)
        aliases = {len(operands): 0}
        operands.append(hidden)
    return call(
        partial(project_kernel, full, half, capacity),
        (
            jax.ShapeDtypeStruct(saved.shape, jnp.bfloat16),
            jax.ShapeDtypeStruct(scores.shape, jnp.float32),
        ),
        (2 * rows.size * units, 2 * (rows.size + weight.size + 2 * count * slots * units)),
        vmem=PROJECT_VMEM,
        grid_spec=pltpu.PrefetchScalarGridSpec(
            num_scalar_prefetch=1,
            in_specs=in_specs,
            out_specs=(outside, inside),
            scratch_shapes=[
                pltpu.VMEM((2, count * slots, features // 2), jnp.bfloat16),
                pltpu.VMEM((2 * slots, LANES), jnp.bfloat16),
                pltpu.VMEM(weight.shape, weight.dtype),
                pltpu.VMEM((count, slots, units), saved.dtype),
                pltpu.VMEM((count * slots, width), jnp.float32),
                pltpu.VMEM((count, slots, units), jnp.bfloat16),
                pltpu.SemaphoreType.DMA((2 * full + 2 * half + 1,)),
                pltpu.SemaphoreType.DMA((units // width,)),
                pltpu.SemaphoreType.DMA((count,)),
                pltpu.SemaphoreType.DMA((units // width * count,)),
            ],
        ),
        input_output_aliases=aliases,
    )(*operands)


def gate_kernel(capacity, scores_ref, routes_ref, affinity_ref, out_ref):
    top = routes_ref.shape[0]
    total, weights = gate_rows(affinity_ref[...])
    labels = iota(scores_ref.shape, 0)
    hits = jnp.zeros(labels.shape, jnp.float32)
    for k in range(top):
        hits += jnp.where(routes_ref[k : k + 1, :] == labels, 1.0, 0.0)
    slot = jnp.where(hits > 0, ranks_before(hits), -1.0).astype(jnp.int32)
    found = jnp.zeros(labels.shape, jnp.float32)
    for r in range(capacity):
        found = jnp.where(slot == r, scores_ref[:, r : r + 1], found)
    place = iota((top, LANES), 0)
    grad = jnp.zeros((top, LANES), jnp.float32)
    for k in range(top):
        line = jnp.sum(jnp.where(routes_ref[k : k + 1, :] == labels, found, 0.0), axis=0, keepdims=True)
        grad = jnp.where(place == k, line, grad)
    weighted = jnp.sum(weights * grad, axis=0, keepdims=True)
    out_ref[...] = (SCALE_ROUTED / total) * grad - weighted / total


def on_device(upstream, routes, affinity, w_down, saved_hidden):
    sections, depth = lax.axis_size("pipe"), lax.axis_size("z")
    section, z, core = lax.axis_index("pipe"), lax.axis_index("z"), lax.axis_index("core")
    everyone = ("z", "x", "core")
    expert_count = depth * COLUMNS * CORES
    local = COLUMNS * CORES
    slot_total, units = saved_hidden.shape[2:]
    capacity = slot_total // expert_count
    tokens, features = upstream.shape[1:]
    half = features // 2
    cores = range(CORES)

    mine = lax.dynamic_slice(upstream[0], (0, core * half), (tokens, half))
    other = lax.dynamic_slice(upstream[0], (0, (1 - core) * half), (tokens, half))
    hop = range(1, sections)
    last = sections - 1
    near = lax.ppermute(mine, ("pipe", "core"), [(i * CORES + c, (i - 1) * CORES + c) for i in hop for c in cores])
    far = lax.ppermute(other, ("pipe", "core"), [(i * CORES + c, (i - 1) * CORES + 1 - c) for i in hop for c in cores])
    stay = lax.ppermute(other, ("pipe", "core"), [(last * CORES + c, last * CORES + 1 - c) for c in cores])

    routes_own = routes[0].T
    affinity_own = affinity[0].T
    choices = jnp.concatenate([routes_own.astype(jnp.float32), affinity_own], 0)
    choices_mate = lax.ppermute(choices, "core", [(c, 1 - c) for c in cores])

    def in_order(a, b, axis):
        return jnp.where(core == 0, jnp.concatenate([a, b], axis), jnp.concatenate([b, a], axis))

    def along(block, distance, cross=False):
        pairs = []
        for i in range(depth):
            pairs.append((i * CORES + (1 if cross else 0), (i + distance) % depth * CORES))
            pairs.append((i * CORES + (0 if cross else 1), (i - distance) % depth * CORES + 1))
        return lax.ppermute(block, ("z", "core"), pairs)

    reach = depth // 2
    choices_at = [in_order(choices, choices_mate, 1)]
    choices_at += [along(choices_at[0], k) for k in range(1, reach + 1)]
    place = jnp.stack([z, core])
    rows = local * CORES * capacity
    inside = pl.BlockSpec(memory_space=pltpu.VMEM)
    onehots, gains, token = call(
        partial(match_kernel, capacity),
        (
            jax.ShapeDtypeStruct((reach + 1, rows, CORES * tokens), jnp.float32),
            jax.ShapeDtypeStruct((reach, rows, LANES), jnp.float32),
            jax.ShapeDtypeStruct((8, LANES), jnp.float32),
        ),
        (10**6, 10**5),
        grid_spec=pltpu.PrefetchScalarGridSpec(
            num_scalar_prefetch=1, in_specs=[inside] * (reach + 1), out_specs=(inside,) * 3
        ),
    )(place, *choices_at)

    def exchange(block, axes, parts):
        shape = block.shape
        block = block.reshape(parts, shape[0] // parts, shape[1])
        return lax.all_to_all(block, axes, split_axis=0, concat_axis=0, tiled=True).reshape(shape)

    near, far, stay, token = lax.optimization_barrier((near, far, stay, token))
    is_last = section == last
    held = in_order(jnp.where(is_last, mine, near), jnp.where(is_last, stay, far), 0)
    weight = w_down[0, 0]
    saved = saved_hidden[0, 0].reshape(depth, slot_total // depth, units)
    scores = jnp.zeros((expert_count, LANES), jnp.float32)

    def at(*distances):
        return jnp.stack([(z + d) % depth for d in distances])

    def columns(blocks, parts, micros):
        rows, after = select_rows(place, onehots, gains, token, blocks, parts, micros)
        return exchange(rows, ("core", "x"), local), after

    groups = []
    same, cross = along(held, 1), along(held, 1, cross=True)
    got, token = columns([held], (0,), COSTS[0])
    groups.append((got, at(0), 0, 1))
    for k in range(1, reach - 1):
        same, cross, token = lax.optimization_barrier((same, cross, token))
        ahead = along(same, 1), along(cross, 1)
        got, token = columns([same, cross], (k, k), COSTS[k])
        groups.append((got, at(-k, k), 1, 0))
        same, cross = ahead
    k = reach - 1
    same, cross, token = lax.optimization_barrier((same, cross, token))
    got, token = columns([same, cross, along(same, 1)], (k, k, k + 1), COSTS[k])
    groups.append((got, at(-k, k, reach), 1, 1))

    hidden = None
    for got, zs, full, part in groups:
        hidden, scores = project(zs, got, weight, saved, scores, hidden, full, part, capacity)

    returned = exchange(scores, everyone, expert_count)
    affinity_grad = call(
        partial(gate_kernel, capacity),
        jax.ShapeDtypeStruct(affinity_own.shape, jnp.float32),
        (10**6, 10**5),
    )(returned, routes_own, affinity_own)
    return hidden.reshape(1, 1, slot_total, units), affinity_grad.T[None]


def solution(mesh):
    sections, experts = mesh.devices.shape
    grid = mesh.devices.reshape(sections, experts // (COLUMNS * CORES), COLUMNS, CORES)
    rows = ("z", "x", "core")
    return jax.shard_map(
        on_device,
        mesh=Mesh(grid, ("pipe",) + rows),
        in_specs=(
            P("pipe", rows, None),
            P("pipe", rows, None),
            P("pipe", rows, None),
            P("pipe", rows, None, None),
            P("pipe", rows, None, None),
        ),
        out_specs=(P("pipe", rows, None, None), P("pipe", rows, None)),
        check_vma=False,
    )
```

```python
from functools import partial

import jax
import jax.numpy as jnp
from jax import lax
from jax.experimental import pallas as pl
from jax.experimental.pallas import tpu as pltpu
from jax.sharding import Mesh, PartitionSpec as P

SCALE_ROUTED = 2.5
CORES = 2
COSTS = 3.0, 3.0, 14.0, 8.0
COLUMNS = 4
LANES = 128
SMALL_VMEM = 12 * 2**20
PROJECT_VMEM = 16 * 2**20


def iota(shape, dim):
    return lax.broadcasted_iota(jnp.int32, shape, dim)


def call(body, out_shape, cost, vmem=SMALL_VMEM, **kwargs):
    return pl.pallas_call(
        body,
        out_shape=out_shape,
        cost_estimate=pl.CostEstimate(flops=cost[0], bytes_accessed=cost[1], transcendentals=0),
        compiler_params=pltpu.CompilerParams(vmem_limit_bytes=vmem),
        **kwargs,
    )


def ranks_before(hits):
    tokens = hits.shape[1]
    first, second = iota((tokens, tokens), 0), iota((tokens, tokens), 1)
    ahead = (first < second) & (first // LANES == second // LANES)
    ahead = jnp.where(ahead, 1.0, 0.0).astype(jnp.bfloat16)
    return jnp.dot(hits.astype(jnp.bfloat16), ahead, preferred_element_type=jnp.float32)


def gate_rows(affinity):
    total = jnp.sum(affinity, axis=0, keepdims=True)
    weights = (SCALE_ROUTED * affinity / total).astype(jnp.bfloat16).astype(jnp.float32)
    return total, weights


def match_kernel(capacity, place_ref, *refs):
    groups = refs[:-3]
    onehot_ref, gain_ref, token_ref = refs[-3:]
    rows, tokens = onehot_ref.shape[1:]
    each = CORES * capacity
    experts = rows // each
    token_ref[...] = jnp.zeros(token_ref.shape, jnp.float32)
    lane = iota((each, LANES), 1)
    last = gain_ref.shape[0] - 1
    for i, group_ref in enumerate(groups):
        top = group_ref.shape[0] // 2
        _, weights = gate_rows(group_ref[top:])
        labels = (place_ref[0] * experts + iota((16, tokens), 0)).astype(jnp.float32)
        hits = jnp.zeros((16, tokens), jnp.float32)
        gains = jnp.zeros((16, tokens), jnp.float32)
        for k in range(top):
            named = group_ref[k : k + 1, :] == labels
            hits += jnp.where(named, 1.0, 0.0)
            gains += jnp.where(named, weights[k : k + 1, :], 0.0)
        slot = ranks_before(hits).astype(jnp.int32) + (iota((16, tokens), 1) // LANES) * capacity
        slot = jnp.where(hits > 0, slot, -1)
        order = iota((each, tokens), 0)
        for at in range(experts):
            s = (at % COLUMNS) * CORES + at // COLUMNS
            found = order == slot[s : s + 1, :]
            here = slice(at * each, (at + 1) * each)
            onehot_ref[i, here] = jnp.where(found, 1.0, 0.0)
            column = jnp.sum(jnp.where(found, gains[s : s + 1, :], 0.0), axis=1, keepdims=True)
            if i <= last:
                gain_ref[i, here] = jnp.where(lane == 0, column, 0.0)
            else:
                gain_ref[last, here] += jnp.where(lane == 1, column, 0.0)


def select_kernel(parts, place_ref, onehot_ref, gain_in, token_ref, *refs):
    blocks = refs[: len(parts)]
    out_hbm, token_out, gain_ref, out_ref, out_sems = refs[len(parts) :]
    count, _, width = out_ref.shape
    tile = width // 2
    first = parts[0]
    token_out[...] = token_ref[...]
    gain_ref[...] = gain_in[first].astype(jnp.bfloat16)
    stores = [pltpu.make_async_copy(gain_ref, out_hbm.at[:, count * width :], out_sems.at[2 * count])]
    stores[0].start()
    for j in range(count):
        onehot = onehot_ref[parts[j]].astype(jnp.bfloat16)
        half = j if count == 1 or j == 2 else jnp.bitwise_xor(j, place_ref[1])
        for h in range(2):
            lanes = slice(h * tile, (h + 1) * tile)
            rows = jnp.dot(onehot, blocks[j][:, lanes], preferred_element_type=jnp.float32)
            out_ref[j, :, lanes] = rows.astype(jnp.bfloat16)
            at = pl.multiple_of(half * width + h * tile, LANES)
            store = pltpu.make_async_copy(
                out_ref.at[j, :, lanes], out_hbm.at[:, pl.ds(at, tile)], out_sems.at[2 * j + h]
            )
            store.start()
            stores.append(store)
    for store in stores:
        store.wait()


def select_rows(place, onehots, gains, token, blocks, parts, micros):
    tokens, width = blocks[0].shape
    rows = onehots.shape[1]
    count = len(blocks)
    outside = pl.BlockSpec(memory_space=pltpu.HBM)
    inside = pl.BlockSpec(memory_space=pltpu.VMEM)
    return call(
        partial(select_kernel, parts),
        (
            jax.ShapeDtypeStruct((rows, width * count + LANES), jnp.bfloat16),
            jax.ShapeDtypeStruct(token.shape, token.dtype),
        ),
        (int(micros * 1.1e9), 2 * (rows + tokens) * width * count),
        grid_spec=pltpu.PrefetchScalarGridSpec(
            num_scalar_prefetch=1,
            in_specs=[inside] * (3 + count),
            out_specs=(outside, inside),
            scratch_shapes=[
                pltpu.VMEM((rows, LANES), jnp.bfloat16),
                pltpu.VMEM((count, rows, width), jnp.bfloat16),
                pltpu.SemaphoreType.DMA((2 * count + 1,)),
            ],
        ),
    )(place, onehots, gains, token, *blocks)


def project_kernel(full, half, capacity, zs_ref, x_ref, w_ref, saved_ref, scores_in, *refs):
    hidden_hbm, scores_ref, y_ref, out_ref, out_sems = refs[-5:]
    blocks, slots, units = out_ref.shape
    features = w_ref.shape[1]
    middle = features // 2
    width = y_ref.shape[1]
    chunks = units // width
    dims = (((1,), (1,)), ((), ()))
    at = features * full
    gain_at = at + middle * half
    def times(x, w):
        return lax.dot_general(x, w, dims, preferred_element_type=jnp.float32)

    row = iota((slots, LANES), 0)
    own_lane = iota((slots, LANES), 1) == row % capacity
    sources = slots // capacity
    scores_ref[...] = scores_in[...]
    gains, totals = [], []
    for j in range(blocks):
        whole = full and j < CORES
        top = j * slots if whole else 0
        lane = 0 if whole or not full else 1
        tile = x_ref[top : top + slots, gain_at : gain_at + LANES].astype(jnp.float32)
        column = tile[:, lane : lane + 1]
        gains.append(jnp.broadcast_to(column, (slots, LANES)))
        totals.append(jnp.zeros((slots, LANES), jnp.float32))

    stores = []
    for n in range(chunks):
        here = slice(n * width, (n + 1) * width)
        if full:
            y_ref[: 2 * slots] = times(x_ref[:, :features], w_ref[here])
        if half:
            y_ref[2 * slots * full :] = times(x_ref[:slots, at : at + middle], w_ref[here, :middle]) + times(
                x_ref[slots:, at : at + middle], w_ref[here, middle:]
            )
        for j in range(blocks):
            for i in range(0, width, LANES):
                lanes = slice(n * width + i, n * width + i + LANES)
                projected = y_ref[j * slots : (j + 1) * slots, i : i + LANES]
                out_ref[j, :, lanes] = (gains[j] * projected).astype(jnp.bfloat16)
                totals[j] += projected * saved_ref[zs_ref[j], :, lanes].astype(jnp.float32)
            store = pltpu.make_async_copy(
                out_ref.at[j, :, here], hidden_hbm.at[zs_ref[j], :, here], out_sems.at[n * blocks + j]
            )
            store.start()
            stores.append(store)

    for j in range(blocks):
        column = jnp.sum(totals[j], axis=1, keepdims=True)
        spread = jnp.where(own_lane, column, 0.0)
        place = iota((sources, LANES), 0)
        table = jnp.zeros((sources, LANES), jnp.float32)
        for s in range(sources):
            line = jnp.sum(jnp.where(row // capacity == s, spread, 0.0), axis=0, keepdims=True)
            table = jnp.where(place == s, line, table)
        scores_ref[pl.ds(pl.multiple_of(zs_ref[j] * sources, sources), sources), :] = table
    for store in stores:
        store.wait()


def project(zs, rows, weight, saved, scores, hidden, full, half, capacity):
    count = CORES * full + half
    blocks, slots, units = saved.shape
    features = weight.shape[1]
    width = 256
    inside = pl.BlockSpec(memory_space=pltpu.VMEM)
    outside = pl.BlockSpec(memory_space=pltpu.HBM)
    in_specs = [inside] * 4
    operands = [zs, rows, weight, saved, scores]
    aliases = {}
    if hidden is not None:
        in_specs.append(outside)
        aliases = {len(operands): 0}
        operands.append(hidden)
    return call(
        partial(project_kernel, full, half, capacity),
        (
            jax.ShapeDtypeStruct(saved.shape, jnp.bfloat16),
            jax.ShapeDtypeStruct(scores.shape, jnp.float32),
        ),
        (2 * rows.size * units, 2 * (rows.size + weight.size + 2 * count * slots * units)),
        vmem=PROJECT_VMEM,
        grid_spec=pltpu.PrefetchScalarGridSpec(
            num_scalar_prefetch=1,
            in_specs=in_specs,
            out_specs=(outside, inside),
            scratch_shapes=[
                pltpu.VMEM((count * slots, width), jnp.float32),
                pltpu.VMEM((count, slots, units), jnp.bfloat16),
                pltpu.SemaphoreType.DMA((units // width * count,)),
            ],
        ),
        input_output_aliases=aliases,
    )(*operands)


def gate_kernel(capacity, scores_ref, routes_ref, affinity_ref, out_ref):
    top = routes_ref.shape[0]
    total, weights = gate_rows(affinity_ref[...])
    labels = iota(scores_ref.shape, 0)
    hits = jnp.zeros(labels.shape, jnp.float32)
    for k in range(top):
        hits += jnp.where(routes_ref[k : k + 1, :] == labels, 1.0, 0.0)
    slot = jnp.where(hits > 0, ranks_before(hits), -1.0).astype(jnp.int32)
    found = jnp.zeros(labels.shape, jnp.float32)
    for r in range(capacity):
        found = jnp.where(slot == r, scores_ref[:, r : r + 1], found)
    place = iota((top, LANES), 0)
    grad = jnp.zeros((top, LANES), jnp.float32)
    for k in range(top):
        line = jnp.sum(jnp.where(routes_ref[k : k + 1, :] == labels, found, 0.0), axis=0, keepdims=True)
        grad = jnp.where(place == k, line, grad)
    weighted = jnp.sum(weights * grad, axis=0, keepdims=True)
    out_ref[...] = (SCALE_ROUTED / total) * grad - weighted / total


def on_device(upstream, routes, affinity, w_down, saved_hidden):
    sections, depth = lax.axis_size("pipe"), lax.axis_size("z")
    section, z, core = lax.axis_index("pipe"), lax.axis_index("z"), lax.axis_index("core")
    everyone = ("z", "x", "core")
    expert_count = depth * COLUMNS * CORES
    local = COLUMNS * CORES
    slot_total, units = saved_hidden.shape[2:]
    capacity = slot_total // expert_count
    tokens, features = upstream.shape[1:]
    half = features // 2
    cores = range(CORES)

    mine = lax.dynamic_slice(upstream[0], (0, core * half), (tokens, half))
    other = lax.dynamic_slice(upstream[0], (0, (1 - core) * half), (tokens, half))
    hop = range(1, sections)
    last = sections - 1
    near = lax.ppermute(mine, ("pipe", "core"), [(i * CORES + c, (i - 1) * CORES + c) for i in hop for c in cores])
    far = lax.ppermute(other, ("pipe", "core"), [(i * CORES + c, (i - 1) * CORES + 1 - c) for i in hop for c in cores])
    stay = lax.ppermute(other, ("pipe", "core"), [(last * CORES + c, last * CORES + 1 - c) for c in cores])

    routes_own = routes[0].T
    affinity_own = affinity[0].T
    choices = jnp.concatenate([routes_own.astype(jnp.float32), affinity_own], 0)
    choices_mate = lax.ppermute(choices, "core", [(c, 1 - c) for c in cores])

    def in_order(a, b, axis):
        return jnp.where(core == 0, jnp.concatenate([a, b], axis), jnp.concatenate([b, a], axis))

    def along(block, distance, cross=False):
        pairs = []
        for i in range(depth):
            pairs.append((i * CORES + (1 if cross else 0), (i + distance) % depth * CORES))
            pairs.append((i * CORES + (0 if cross else 1), (i - distance) % depth * CORES + 1))
        return lax.ppermute(block, ("z", "core"), pairs)

    reach = depth // 2
    place = jnp.stack([z, core])
    rows = local * CORES * capacity
    inside = pl.BlockSpec(memory_space=pltpu.VMEM)

    def match(choices_at):
        count = len(choices_at)
        return call(
            partial(match_kernel, capacity),
            (
                jax.ShapeDtypeStruct((count, rows, CORES * tokens), jnp.float32),
                jax.ShapeDtypeStruct((max(1, count - 1), rows, LANES), jnp.float32),
                jax.ShapeDtypeStruct((8, LANES), jnp.float32),
            ),
            (10**6, 10**5),
            grid_spec=pltpu.PrefetchScalarGridSpec(
                num_scalar_prefetch=1, in_specs=[inside] * count, out_specs=(inside,) * 3
            ),
        )(place, *choices_at)

    choices = in_order(choices, choices_mate, 1)
    onehots, gains, token = match([choices])

    def exchange(block, axes, parts):
        shape = block.shape
        block = block.reshape(parts, shape[0] // parts, shape[1])
        return lax.all_to_all(block, axes, split_axis=0, concat_axis=0, tiled=True).reshape(shape)

    near, far, stay, token = lax.optimization_barrier((near, far, stay, token))
    is_last = section == last
    held = in_order(jnp.where(is_last, mine, near), jnp.where(is_last, stay, far), 0)
    weight = w_down[0, 0]
    saved = saved_hidden[0, 0].reshape(depth, slot_total // depth, units)
    scores = jnp.zeros((expert_count, LANES), jnp.float32)

    def at(*distances):
        return jnp.stack([(z + d) % depth for d in distances])

    def columns(onehots, gains, token, blocks, parts, micros):
        rows, after = select_rows(place, onehots, gains, token, blocks, parts, micros)
        return exchange(rows, ("core", "x"), local), after

    groups = []
    same, cross = along(held, 1), along(held, 1, cross=True)
    got, token = columns(onehots, gains, token, [held], (0,), COSTS[0])
    choices, token = lax.optimization_barrier((choices, token))
    onehots, gains, matched = match([along(choices, k) for k in range(1, reach + 1)])
    token += matched
    groups.append((got, at(0), 0, 1))
    for k in range(1, reach - 1):
        same, cross, token = lax.optimization_barrier((same, cross, token))
        ahead = along(same, 1), along(cross, 1)
        got, token = columns(onehots, gains, token, [same, cross], (k - 1, k - 1), COSTS[k])
        groups.append((got, at(-k, k), 1, 0))
        same, cross = ahead
    k = reach - 1
    same, cross, token = lax.optimization_barrier((same, cross, token))
    got, token = columns(onehots, gains, token, [same, cross, along(same, 1)], (k - 1, k - 1, k), COSTS[k])
    groups.append((got, at(-k, k, reach), 1, 1))

    hidden = None
    for got, zs, full, part in groups:
        hidden, scores = project(zs, got, weight, saved, scores, hidden, full, part, capacity)

    returned = exchange(scores, everyone, expert_count)
    affinity_grad = call(
        partial(gate_kernel, capacity),
        jax.ShapeDtypeStruct(affinity_own.shape, jnp.float32),
        (10**6, 10**5),
    )(returned, routes_own, affinity_own)
    return hidden.reshape(1, 1, slot_total, units), affinity_grad.T[None]


def solution(mesh):
    sections, experts = mesh.devices.shape
    grid = mesh.devices.reshape(sections, experts // (COLUMNS * CORES), COLUMNS, CORES)
    rows = ("z", "x", "core")
    return jax.shard_map(
        on_device,
        mesh=Mesh(grid, ("pipe",) + rows),
        in_specs=(
            P("pipe", rows, None),
            P("pipe", rows, None),
            P("pipe", rows, None),
            P("pipe", rows, None, None),
            P("pipe", rows, None, None),
        ),
        out_specs=(P("pipe", rows, None, None), P("pipe", rows, None)),
        check_vma=False,
    )
```

```python
from functools import partial

import jax
import jax.numpy as jnp
from jax import lax
from jax.experimental import pallas as pl
from jax.experimental.pallas import tpu as pltpu
from jax.sharding import Mesh, PartitionSpec as P

SCALE_ROUTED = 2.5
CORES = 2
WIDTH = 512
COSTS = 3.0, 3.0, 14.0, 8.0
COLUMNS = 4
LANES = 128
SMALL_VMEM = 12 * 2**20
PROJECT_VMEM = 57 * 2**20


def iota(shape, dim):
    return lax.broadcasted_iota(jnp.int32, shape, dim)


def call(body, out_shape, cost, vmem=SMALL_VMEM, **kwargs):
    return pl.pallas_call(
        body,
        out_shape=out_shape,
        cost_estimate=pl.CostEstimate(flops=cost[0], bytes_accessed=cost[1], transcendentals=0),
        compiler_params=pltpu.CompilerParams(vmem_limit_bytes=vmem),
        **kwargs,
    )


def ranks_before(hits):
    tokens = hits.shape[1]
    first, second = iota((tokens, tokens), 0), iota((tokens, tokens), 1)
    ahead = (first < second) & (first // LANES == second // LANES)
    ahead = jnp.where(ahead, 1.0, 0.0).astype(jnp.bfloat16)
    return jnp.dot(hits.astype(jnp.bfloat16), ahead, preferred_element_type=jnp.float32)


def gate_rows(affinity):
    total = jnp.sum(affinity, axis=0, keepdims=True)
    weights = (SCALE_ROUTED * affinity / total).astype(jnp.bfloat16).astype(jnp.float32)
    return total, weights


def matches(group_ref, z, experts, each):
    top, tokens = group_ref.shape[0] // 2, group_ref.shape[1]
    _, weights = gate_rows(group_ref[top:])
    labels = (z * experts + iota((16, tokens), 0)).astype(jnp.float32)
    hits = jnp.zeros((16, tokens), jnp.float32)
    gains = jnp.zeros((16, tokens), jnp.float32)
    for k in range(top):
        named = group_ref[k : k + 1, :] == labels
        hits += jnp.where(named, 1.0, 0.0)
        gains += jnp.where(named, weights[k : k + 1, :], 0.0)
    slot = ranks_before(hits).astype(jnp.int32) + (iota((16, tokens), 1) // LANES) * (each // CORES)
    slot = jnp.where(hits > 0, slot, -1)
    order = iota((each, tokens), 0)
    lines, columns = [], []
    for at in range(experts):
        s = (at % COLUMNS) * CORES + at // COLUMNS
        found = order == slot[s : s + 1, :]
        lines.append(jnp.where(found, 1.0, 0.0))
        columns.append(jnp.sum(jnp.where(found, gains[s : s + 1, :], 0.0), axis=1, keepdims=True))
    return jnp.concatenate(lines, axis=0).astype(jnp.bfloat16), jnp.concatenate(columns, axis=0)


def select_kernel(parts, capacity, place_ref, token_ref, *refs):
    groups = refs[: max(parts) + 1]
    blocks = refs[len(groups) : len(groups) + len(parts)]
    out_hbm, token_out, gain_ref, out_ref, out_sems = refs[-5:]
    count, rows, width = out_ref.shape
    tile = width // 2
    each = CORES * capacity
    token_out[...] = token_ref[...]
    found = [matches(group_ref, place_ref[0], rows // each, each) for group_ref in groups]
    stores = []
    for j in range(count):
        half = j if count == 1 or j == 2 else jnp.bitwise_xor(j, place_ref[1])
        for h in range(2):
            lanes = slice(h * tile, (h + 1) * tile)
            picked = jnp.dot(found[parts[j]][0], blocks[j][:, lanes], preferred_element_type=jnp.float32)
            out_ref[j, :, lanes] = picked.astype(jnp.bfloat16)
            at = pl.multiple_of(half * width + h * tile, LANES)
            store = pltpu.make_async_copy(
                out_ref.at[j, :, lanes], out_hbm.at[:, pl.ds(at, tile)], out_sems.at[2 * j + h]
            )
            store.start()
            stores.append(store)
    lane = iota((rows, LANES), 1)
    table = jnp.zeros((rows, LANES), jnp.float32)
    for i, (_, column) in enumerate(found):
        table = jnp.where(lane == i, column, table)
    gain_ref[...] = table.astype(jnp.bfloat16)
    store = pltpu.make_async_copy(gain_ref, out_hbm.at[:, count * width :], out_sems.at[2 * count])
    store.start()
    for store in stores + [store]:
        store.wait()


def select_rows(place, token, groups, blocks, parts, rows, capacity, micros):
    tokens, width = blocks[0].shape
    count = len(blocks)
    outside = pl.BlockSpec(memory_space=pltpu.HBM)
    inside = pl.BlockSpec(memory_space=pltpu.VMEM)
    return call(
        partial(select_kernel, parts, capacity),
        (
            jax.ShapeDtypeStruct((rows, width * count + LANES), jnp.bfloat16),
            jax.ShapeDtypeStruct(token.shape, token.dtype),
        ),
        (int(micros * 1.1e9), 2 * (rows + tokens) * width * count),
        grid_spec=pltpu.PrefetchScalarGridSpec(
            num_scalar_prefetch=1,
            in_specs=[inside] * (1 + len(groups) + count),
            out_specs=(outside, inside),
            scratch_shapes=[
                pltpu.VMEM((rows, LANES), jnp.bfloat16),
                pltpu.VMEM((count, rows, width), jnp.bfloat16),
                pltpu.SemaphoreType.DMA((2 * count + 1,)),
            ],
        ),
    )(place, token, *groups, *blocks)


def project_kernel(full, half, capacity, zs_ref, x_ref, w_ref, *refs):
    count = CORES * full + half
    saved, scores_in = refs[:count], refs[count]
    hidden_hbm, scores_ref, y_ref, out_ref, total_ref, out_sems = refs[-6:]
    n, chunks = pl.program_id(0), out_ref.shape[0]
    slots, width = out_ref.shape[2:]
    features = w_ref.shape[1]
    middle = features // 2
    at = features * full
    gain_at = at + middle * half
    dims = (((1,), (1,)), ((), ()))

    def times(x, w):
        return lax.dot_general(x, w, dims, preferred_element_type=jnp.float32)

    def store(step, j):
        lanes = pl.ds(pl.multiple_of(step * width, LANES), width)
        return pltpu.make_async_copy(
            out_ref.at[step, j], hidden_hbm.at[zs_ref[j], :, lanes], out_sems.at[step, j]
        )

    @pl.when(n == 0)
    def _():
        total_ref[...] = jnp.zeros(total_ref.shape, jnp.float32)
        scores_ref[...] = scores_in[...]

    if full:
        y_ref[: 2 * slots] = times(x_ref[:, :features], w_ref[...])
    if half:
        y_ref[2 * slots * full :] = times(x_ref[:slots, at : at + middle], w_ref[:, :middle]) + times(
            x_ref[slots:, at : at + middle], w_ref[:, middle:]
        )
    for j in range(count):
        whole = full and j < CORES
        top = j * slots if whole else 0
        lane = 0 if whole or not full else 1
        tile = x_ref[top : top + slots, gain_at : gain_at + LANES].astype(jnp.float32)
        gain = jnp.broadcast_to(tile[:, lane : lane + 1], (slots, LANES))
        total = total_ref[j]
        for i in range(0, width, LANES):
            lanes = slice(i, i + LANES)
            projected = y_ref[j * slots : (j + 1) * slots, lanes]
            out_ref[n, j, :, lanes] = (gain * projected).astype(jnp.bfloat16)
            total += projected * saved[j][0, :, lanes].astype(jnp.float32)
        total_ref[j] = total
        store(n, j).start()

    @pl.when(n == chunks - 1)
    def _():
        row = iota((slots, LANES), 0)
        own_lane = iota((slots, LANES), 1) == row % capacity
        sources = slots // capacity
        place = iota((sources, LANES), 0)
        for j in range(count):
            column = jnp.sum(total_ref[j], axis=1, keepdims=True)
            spread = jnp.where(own_lane, column, 0.0)
            table = jnp.zeros((sources, LANES), jnp.float32)
            for s in range(sources):
                line = jnp.sum(jnp.where(row // capacity == s, spread, 0.0), axis=0, keepdims=True)
                table = jnp.where(place == s, line, table)
            scores_ref[pl.ds(pl.multiple_of(zs_ref[j] * sources, sources), sources), :] = table
        for step in range(chunks):
            for j in range(count):
                store(step, j).wait()


def project(zs, rows, weight, saved, scores, hidden, full, half, capacity):
    count = CORES * full + half
    blocks, slots, units = saved.shape
    width = WIDTH
    chunks = units // width
    whole = lambda n, zs: (0, 0)
    inside = pl.BlockSpec(memory_space=pltpu.VMEM)
    outside = pl.BlockSpec(memory_space=pltpu.HBM)
    in_specs = [inside, pl.BlockSpec((width, weight.shape[1]), lambda n, zs: (n, 0))]
    in_specs += [pl.BlockSpec((1, slots, width), lambda n, zs, j=j: (zs[j], 0, n)) for j in range(count)]
    in_specs += [pl.BlockSpec(scores.shape, whole)]
    operands = [zs, rows, weight] + [saved] * count + [scores]
    aliases = {}
    if hidden is not None:
        in_specs.append(outside)
        aliases = {len(operands): 0}
        operands.append(hidden)
    return call(
        partial(project_kernel, full, half, capacity),
        (
            jax.ShapeDtypeStruct(saved.shape, jnp.bfloat16),
            jax.ShapeDtypeStruct(scores.shape, jnp.float32),
        ),
        (2 * rows.size * units, 2 * (rows.size + weight.size + 2 * count * slots * units)),
        vmem=PROJECT_VMEM,
        grid_spec=pltpu.PrefetchScalarGridSpec(
            num_scalar_prefetch=1,
            grid=(chunks,),
            in_specs=in_specs,
            out_specs=(outside, pl.BlockSpec(scores.shape, whole)),
            scratch_shapes=[
                pltpu.VMEM((count * slots, width), jnp.float32),
                pltpu.VMEM((chunks, count, slots, width), jnp.bfloat16),
                pltpu.VMEM((count, slots, LANES), jnp.float32),
                pltpu.SemaphoreType.DMA((chunks, count)),
            ],
        ),
        input_output_aliases=aliases,
    )(*operands)


def gate_kernel(capacity, scores_ref, routes_ref, affinity_ref, out_ref):
    top = routes_ref.shape[0]
    total, weights = gate_rows(affinity_ref[...])
    labels = iota(scores_ref.shape, 0)
    hits = jnp.zeros(labels.shape, jnp.float32)
    for k in range(top):
        hits += jnp.where(routes_ref[k : k + 1, :] == labels, 1.0, 0.0)
    slot = jnp.where(hits > 0, ranks_before(hits), -1.0).astype(jnp.int32)
    found = jnp.zeros(labels.shape, jnp.float32)
    for r in range(capacity):
        found = jnp.where(slot == r, scores_ref[:, r : r + 1], found)
    place = iota((top, LANES), 0)
    grad = jnp.zeros((top, LANES), jnp.float32)
    for k in range(top):
        line = jnp.sum(jnp.where(routes_ref[k : k + 1, :] == labels, found, 0.0), axis=0, keepdims=True)
        grad = jnp.where(place == k, line, grad)
    weighted = jnp.sum(weights * grad, axis=0, keepdims=True)
    out_ref[...] = (SCALE_ROUTED / total) * grad - weighted / total


def on_device(upstream, routes, affinity, w_down, saved_hidden):
    sections, depth = lax.axis_size("pipe"), lax.axis_size("z")
    section, z, core = lax.axis_index("pipe"), lax.axis_index("z"), lax.axis_index("core")
    everyone = ("z", "x", "core")
    expert_count = depth * COLUMNS * CORES
    local = COLUMNS * CORES
    slot_total, units = saved_hidden.shape[2:]
    capacity = slot_total // expert_count
    tokens, features = upstream.shape[1:]
    half = features // 2
    cores = range(CORES)

    mine = lax.dynamic_slice(upstream[0], (0, core * half), (tokens, half))
    other = lax.dynamic_slice(upstream[0], (0, (1 - core) * half), (tokens, half))
    hop = range(1, sections)
    last = sections - 1
    near = lax.ppermute(mine, ("pipe", "core"), [(i * CORES + c, (i - 1) * CORES + c) for i in hop for c in cores])
    far = lax.ppermute(other, ("pipe", "core"), [(i * CORES + c, (i - 1) * CORES + 1 - c) for i in hop for c in cores])
    stay = lax.ppermute(other, ("pipe", "core"), [(last * CORES + c, last * CORES + 1 - c) for c in cores])

    routes_own = routes[0].T
    affinity_own = affinity[0].T
    choices = jnp.concatenate([routes_own.astype(jnp.float32), affinity_own], 0)
    choices_mate = lax.ppermute(choices, "core", [(c, 1 - c) for c in cores])

    def in_order(a, b, axis):
        return jnp.where(core == 0, jnp.concatenate([a, b], axis), jnp.concatenate([b, a], axis))

    def along(block, distance, cross=False):
        pairs = []
        for i in range(depth):
            pairs.append((i * CORES + (1 if cross else 0), (i + distance) % depth * CORES))
            pairs.append((i * CORES + (0 if cross else 1), (i - distance) % depth * CORES + 1))
        return lax.ppermute(block, ("z", "core"), pairs)

    reach = depth // 2
    place = jnp.stack([z, core])
    rows = local * CORES * capacity
    choices = [in_order(choices, choices_mate, 1)]
    choices += [along(choices[0], k) for k in range(1, reach + 1)]
    token = jnp.zeros((8, LANES), jnp.float32)

    def exchange(block, axes, parts):
        shape = block.shape
        block = block.reshape(parts, shape[0] // parts, shape[1])
        return lax.all_to_all(block, axes, split_axis=0, concat_axis=0, tiled=True).reshape(shape)

    near, far, stay, choices = lax.optimization_barrier((near, far, stay, choices))
    is_last = section == last
    held = in_order(jnp.where(is_last, mine, near), jnp.where(is_last, stay, far), 0)
    weight = w_down[0, 0]
    saved = saved_hidden[0, 0].reshape(depth, slot_total // depth, units)
    scores = jnp.zeros((expert_count, LANES), jnp.float32)

    def at(*distances):
        return jnp.stack([(z + d) % depth for d in distances])

    def columns(groups, blocks, parts, micros):
        picked, after = select_rows(place, token, groups, blocks, parts, rows, capacity, micros)
        return exchange(picked, ("core", "x"), local), after

    groups = []
    same, cross = along(held, 1), along(held, 1, cross=True)
    got, token = columns(choices[:1], [held], (0,), COSTS[0])
    groups.append((got, at(0), 0, 1))
    for k in range(1, reach - 1):
        same, cross, token = lax.optimization_barrier((same, cross, token))
        ahead = along(same, 1), along(cross, 1)
        got, token = columns([choices[k]], [same, cross], (0, 0), COSTS[k])
        groups.append((got, at(-k, k), 1, 0))
        same, cross = ahead
    k = reach - 1
    same, cross, token = lax.optimization_barrier((same, cross, token))
    got, token = columns(choices[k:], [same, cross, along(same, 1)], (0, 0, 1), COSTS[k])
    groups.append((got, at(-k, k, reach), 1, 1))

    hidden = None
    for got, zs, full, part in groups:
        hidden, scores = project(zs, got, weight, saved, scores, hidden, full, part, capacity)

    returned = exchange(scores, everyone, expert_count)
    affinity_grad = call(
        partial(gate_kernel, capacity),
        jax.ShapeDtypeStruct(affinity_own.shape, jnp.float32),
        (10**6, 10**5),
    )(returned, routes_own, affinity_own)
    return hidden.reshape(1, 1, slot_total, units), affinity_grad.T[None]


def solution(mesh):
    sections, experts = mesh.devices.shape
    grid = mesh.devices.reshape(sections, experts // (COLUMNS * CORES), COLUMNS, CORES)
    rows = ("z", "x", "core")
    return jax.shard_map(
        on_device,
        mesh=Mesh(grid, ("pipe",) + rows),
        in_specs=(
            P("pipe", rows, None),
            P("pipe", rows, None),
            P("pipe", rows, None),
            P("pipe", rows, None, None),
            P("pipe", rows, None, None),
        ),
        out_specs=(P("pipe", rows, None, None), P("pipe", rows, None)),
        check_vma=False,
    )
```

```python
from functools import partial

import jax
import jax.numpy as jnp
from jax import lax
from jax.experimental import pallas as pl
from jax.experimental.pallas import tpu as pltpu
from jax.sharding import Mesh, PartitionSpec as P

SCALE_ROUTED = 2.5
CORES = 2
WIDTH = 512
COSTS = 3.0, 3.0, 14.0, 8.0
COLUMNS = 4
LANES = 128
SMALL_VMEM = 12 * 2**20
PROJECT_VMEM = 57 * 2**20
LAST_VMEM = 48 * 2**20


def iota(shape, dim):
    return lax.broadcasted_iota(jnp.int32, shape, dim)


def call(body, out_shape, cost, vmem=SMALL_VMEM, **kwargs):
    return pl.pallas_call(
        body,
        out_shape=out_shape,
        cost_estimate=pl.CostEstimate(flops=cost[0], bytes_accessed=cost[1], transcendentals=0),
        compiler_params=pltpu.CompilerParams(vmem_limit_bytes=vmem),
        **kwargs,
    )


def ranks_before(hits):
    tokens = hits.shape[1]
    first, second = iota((tokens, tokens), 0), iota((tokens, tokens), 1)
    ahead = (first < second) & (first // LANES == second // LANES)
    ahead = jnp.where(ahead, 1.0, 0.0).astype(jnp.bfloat16)
    return jnp.dot(hits.astype(jnp.bfloat16), ahead, preferred_element_type=jnp.float32)


def gate_rows(affinity):
    total = jnp.sum(affinity, axis=0, keepdims=True)
    weights = (SCALE_ROUTED * affinity / total).astype(jnp.bfloat16).astype(jnp.float32)
    return total, weights


def matches(group_ref, z, experts, each):
    top, tokens = group_ref.shape[0] // 2, group_ref.shape[1]
    _, weights = gate_rows(group_ref[top:])
    labels = (z * experts + iota((16, tokens), 0)).astype(jnp.float32)
    hits = jnp.zeros((16, tokens), jnp.float32)
    gains = jnp.zeros((16, tokens), jnp.float32)
    for k in range(top):
        named = group_ref[k : k + 1, :] == labels
        hits += jnp.where(named, 1.0, 0.0)
        gains += jnp.where(named, weights[k : k + 1, :], 0.0)
    slot = ranks_before(hits).astype(jnp.int32) + (iota((16, tokens), 1) // LANES) * (each // CORES)
    slot = jnp.where(hits > 0, slot, -1)
    order = iota((each, tokens), 0)
    lines, columns = [], []
    for at in range(experts):
        s = (at % COLUMNS) * CORES + at // COLUMNS
        found = order == slot[s : s + 1, :]
        lines.append(jnp.where(found, 1.0, 0.0))
        columns.append(jnp.sum(jnp.where(found, gains[s : s + 1, :], 0.0), axis=1, keepdims=True))
    return jnp.concatenate(lines, axis=0).astype(jnp.bfloat16), jnp.concatenate(columns, axis=0)


def select_kernel(parts, capacity, place_ref, token_ref, *refs):
    groups = refs[: max(parts) + 1]
    blocks = refs[len(groups) : len(groups) + len(parts)]
    out_hbm, token_out, gain_ref, out_ref, out_sems = refs[-5:]
    count, rows, width = out_ref.shape
    tile = width // 2
    each = CORES * capacity
    token_out[...] = token_ref[...]
    found = [matches(group_ref, place_ref[0], rows // each, each) for group_ref in groups]
    stores = []
    for j in range(count):
        half = j if count == 1 or j == 2 else jnp.bitwise_xor(j, place_ref[1])
        for h in range(2):
            lanes = slice(h * tile, (h + 1) * tile)
            picked = jnp.dot(found[parts[j]][0], blocks[j][:, lanes], preferred_element_type=jnp.float32)
            out_ref[j, :, lanes] = picked.astype(jnp.bfloat16)
            at = pl.multiple_of(half * width + h * tile, LANES)
            store = pltpu.make_async_copy(
                out_ref.at[j, :, lanes], out_hbm.at[:, pl.ds(at, tile)], out_sems.at[2 * j + h]
            )
            store.start()
            stores.append(store)
    lane = iota((rows, LANES), 1)
    table = jnp.zeros((rows, LANES), jnp.float32)
    for i, (_, column) in enumerate(found):
        table = jnp.where(lane == i, column, table)
    gain_ref[...] = table.astype(jnp.bfloat16)
    store = pltpu.make_async_copy(gain_ref, out_hbm.at[:, count * width :], out_sems.at[2 * count])
    store.start()
    for store in stores + [store]:
        store.wait()


def select_rows(place, token, groups, blocks, parts, rows, capacity, micros):
    tokens, width = blocks[0].shape
    count = len(blocks)
    outside = pl.BlockSpec(memory_space=pltpu.HBM)
    inside = pl.BlockSpec(memory_space=pltpu.VMEM)
    return call(
        partial(select_kernel, parts, capacity),
        (
            jax.ShapeDtypeStruct((rows, width * count + LANES), jnp.bfloat16),
            jax.ShapeDtypeStruct(token.shape, token.dtype),
        ),
        (int(micros * 1.1e9), 2 * (rows + tokens) * width * count),
        grid_spec=pltpu.PrefetchScalarGridSpec(
            num_scalar_prefetch=1,
            in_specs=[inside] * (1 + len(groups) + count),
            out_specs=(outside, inside),
            scratch_shapes=[
                pltpu.VMEM((rows, LANES), jnp.bfloat16),
                pltpu.VMEM((count, rows, width), jnp.bfloat16),
                pltpu.SemaphoreType.DMA((2 * count + 1,)),
            ],
        ),
    )(place, token, *groups, *blocks)


def project_kernel(full, half, capacity, zs_ref, x_ref, w_ref, *refs):
    count = CORES * full + half
    saved, scores_in = refs[:count], refs[count]
    hidden_hbm, scores_ref, y_ref, out_ref, total_ref, out_sems = refs[-6:]
    n, chunks = pl.program_id(0), out_ref.shape[0]
    slots, width = out_ref.shape[2:]
    features = w_ref.shape[1]
    middle = features // 2
    at = features * full
    gain_at = at + middle * half
    dims = (((1,), (1,)), ((), ()))

    def times(x, w):
        return lax.dot_general(x, w, dims, preferred_element_type=jnp.float32)

    def store(step, j):
        lanes = pl.ds(pl.multiple_of(step * width, LANES), width)
        return pltpu.make_async_copy(
            out_ref.at[step, j], hidden_hbm.at[zs_ref[j], :, lanes], out_sems.at[step, j]
        )

    @pl.when(n == 0)
    def _():
        total_ref[...] = jnp.zeros(total_ref.shape, jnp.float32)
        scores_ref[...] = scores_in[...]

    if full:
        y_ref[: 2 * slots] = times(x_ref[:, :features], w_ref[...])
    if half:
        y_ref[2 * slots * full :] = times(x_ref[:slots, at : at + middle], w_ref[:, :middle]) + times(
            x_ref[slots:, at : at + middle], w_ref[:, middle:]
        )
    for j in range(count):
        whole = full and j < CORES
        top = j * slots if whole else 0
        lane = 0 if whole or not full else 1
        tile = x_ref[top : top + slots, gain_at : gain_at + LANES].astype(jnp.float32)
        gain = jnp.broadcast_to(tile[:, lane : lane + 1], (slots, LANES))
        total = total_ref[j]
        for i in range(0, width, LANES):
            lanes = slice(i, i + LANES)
            projected = y_ref[j * slots : (j + 1) * slots, lanes]
            out_ref[n, j, :, lanes] = (gain * projected).astype(jnp.bfloat16)
            total += projected * saved[j][0, :, lanes].astype(jnp.float32)
        total_ref[j] = total
        store(n, j).start()

    @pl.when(n == chunks - 1)
    def _():
        row = iota((slots, LANES), 0)
        own_lane = iota((slots, LANES), 1) == row % capacity
        sources = slots // capacity
        place = iota((sources, LANES), 0)
        for j in range(count):
            column = jnp.sum(total_ref[j], axis=1, keepdims=True)
            spread = jnp.where(own_lane, column, 0.0)
            table = jnp.zeros((sources, LANES), jnp.float32)
            for s in range(sources):
                line = jnp.sum(jnp.where(row // capacity == s, spread, 0.0), axis=0, keepdims=True)
                table = jnp.where(place == s, line, table)
            scores_ref[pl.ds(pl.multiple_of(zs_ref[j] * sources, sources), sources), :] = table
        for step in range(chunks):
            for j in range(count):
                store(step, j).wait()


def project(zs, rows, weight, saved, scores, hidden, full, half, capacity):
    count = CORES * full + half
    blocks, slots, units = saved.shape
    width = WIDTH
    chunks = units // width
    whole = lambda n, zs: (0, 0)
    inside = pl.BlockSpec(memory_space=pltpu.VMEM)
    outside = pl.BlockSpec(memory_space=pltpu.HBM)
    in_specs = [inside, pl.BlockSpec((width, weight.shape[1]), lambda n, zs: (n, 0))]
    in_specs += [pl.BlockSpec((1, slots, width), lambda n, zs, j=j: (zs[j], 0, n)) for j in range(count)]
    in_specs += [pl.BlockSpec(scores.shape, whole)]
    operands = [zs, rows, weight] + [saved] * count + [scores]
    aliases = {}
    if hidden is not None:
        in_specs.append(outside)
        aliases = {len(operands): 0}
        operands.append(hidden)
    return call(
        partial(project_kernel, full, half, capacity),
        (
            jax.ShapeDtypeStruct(saved.shape, jnp.bfloat16),
            jax.ShapeDtypeStruct(scores.shape, jnp.float32),
        ),
        (2 * rows.size * units, 2 * (rows.size + weight.size + 2 * count * slots * units)),
        vmem=LAST_VMEM if full and half else PROJECT_VMEM,
        grid_spec=pltpu.PrefetchScalarGridSpec(
            num_scalar_prefetch=1,
            grid=(chunks,),
            in_specs=in_specs,
            out_specs=(outside, pl.BlockSpec(scores.shape, whole)),
            scratch_shapes=[
                pltpu.VMEM((count * slots, width), jnp.float32),
                pltpu.VMEM((chunks, count, slots, width), jnp.bfloat16),
                pltpu.VMEM((count, slots, LANES), jnp.float32),
                pltpu.SemaphoreType.DMA((chunks, count)),
            ],
        ),
        input_output_aliases=aliases,
    )(*operands)


def gate_kernel(capacity, scores_ref, routes_ref, affinity_ref, out_ref):
    top = routes_ref.shape[0]
    total, weights = gate_rows(affinity_ref[...])
    labels = iota(scores_ref.shape, 0)
    hits = jnp.zeros(labels.shape, jnp.float32)
    for k in range(top):
        hits += jnp.where(routes_ref[k : k + 1, :] == labels, 1.0, 0.0)
    slot = jnp.where(hits > 0, ranks_before(hits), -1.0).astype(jnp.int32)
    found = jnp.zeros(labels.shape, jnp.float32)
    for r in range(capacity):
        found = jnp.where(slot == r, scores_ref[:, r : r + 1], found)
    place = iota((top, LANES), 0)
    grad = jnp.zeros((top, LANES), jnp.float32)
    for k in range(top):
        line = jnp.sum(jnp.where(routes_ref[k : k + 1, :] == labels, found, 0.0), axis=0, keepdims=True)
        grad = jnp.where(place == k, line, grad)
    weighted = jnp.sum(weights * grad, axis=0, keepdims=True)
    out_ref[...] = (SCALE_ROUTED / total) * grad - weighted / total


def on_device(upstream, routes, affinity, w_down, saved_hidden):
    sections, depth = lax.axis_size("pipe"), lax.axis_size("z")
    section, z, core = lax.axis_index("pipe"), lax.axis_index("z"), lax.axis_index("core")
    everyone = ("z", "x", "core")
    expert_count = depth * COLUMNS * CORES
    local = COLUMNS * CORES
    slot_total, units = saved_hidden.shape[2:]
    capacity = slot_total // expert_count
    tokens, features = upstream.shape[1:]
    half = features // 2
    cores = range(CORES)

    mine = lax.dynamic_slice(upstream[0], (0, core * half), (tokens, half))
    other = lax.dynamic_slice(upstream[0], (0, (1 - core) * half), (tokens, half))
    hop = range(1, sections)
    last = sections - 1
    near = lax.ppermute(mine, ("pipe", "core"), [(i * CORES + c, (i - 1) * CORES + c) for i in hop for c in cores])
    far = lax.ppermute(other, ("pipe", "core"), [(i * CORES + c, (i - 1) * CORES + 1 - c) for i in hop for c in cores])
    stay = lax.ppermute(other, ("pipe", "core"), [(last * CORES + c, last * CORES + 1 - c) for c in cores])

    routes_own = routes[0].T
    affinity_own = affinity[0].T
    choices = jnp.concatenate([routes_own.astype(jnp.float32), affinity_own], 0)
    choices_mate = lax.ppermute(choices, "core", [(c, 1 - c) for c in cores])

    def in_order(a, b, axis):
        return jnp.where(core == 0, jnp.concatenate([a, b], axis), jnp.concatenate([b, a], axis))

    def along(block, distance, cross=False):
        pairs = []
        for i in range(depth):
            pairs.append((i * CORES + (1 if cross else 0), (i + distance) % depth * CORES))
            pairs.append((i * CORES + (0 if cross else 1), (i - distance) % depth * CORES + 1))
        return lax.ppermute(block, ("z", "core"), pairs)

    reach = depth // 2
    place = jnp.stack([z, core])
    rows = local * CORES * capacity
    choices = [in_order(choices, choices_mate, 1)]
    choices += [along(choices[0], k) for k in range(1, reach + 1)]
    token = jnp.zeros((8, LANES), jnp.float32)

    def exchange(block, axes, parts):
        shape = block.shape
        block = block.reshape(parts, shape[0] // parts, shape[1])
        return lax.all_to_all(block, axes, split_axis=0, concat_axis=0, tiled=True).reshape(shape)

    near, far, stay, choices = lax.optimization_barrier((near, far, stay, choices))
    is_last = section == last
    held = in_order(jnp.where(is_last, mine, near), jnp.where(is_last, stay, far), 0)
    weight = w_down[0, 0]
    saved = saved_hidden[0, 0].reshape(depth, slot_total // depth, units)
    scores = jnp.zeros((expert_count, LANES), jnp.float32)

    def at(*distances):
        return jnp.stack([(z + d) % depth for d in distances])

    def columns(groups, blocks, parts, micros):
        picked, after = select_rows(place, token, groups, blocks, parts, rows, capacity, micros)
        return exchange(picked, ("core", "x"), local), after

    groups = []
    same, cross = along(held, 1), along(held, 1, cross=True)
    got, token = columns(choices[:1], [held], (0,), COSTS[0])
    groups.append((got, at(0), 0, 1))
    for k in range(1, reach - 1):
        same, cross, token = lax.optimization_barrier((same, cross, token))
        ahead = along(same, 1), along(cross, 1)
        got, token = columns([choices[k]], [same, cross], (0, 0), COSTS[k])
        groups.append((got, at(-k, k), 1, 0))
        same, cross = ahead
    k = reach - 1
    same, cross, token = lax.optimization_barrier((same, cross, token))
    got, token = columns(choices[k:], [same, cross, along(same, 1)], (0, 0, 1), COSTS[k])
    groups.append((got, at(-k, k, reach), 1, 1))

    hidden = None
    for got, zs, full, part in groups:
        hidden, scores = project(zs, got, weight, saved, scores, hidden, full, part, capacity)

    returned = exchange(scores, everyone, expert_count)
    affinity_grad = call(
        partial(gate_kernel, capacity),
        jax.ShapeDtypeStruct(affinity_own.shape, jnp.float32),
        (10**6, 10**5),
    )(returned, routes_own, affinity_own)
    return hidden.reshape(1, 1, slot_total, units), affinity_grad.T[None]


def solution(mesh):
    sections, experts = mesh.devices.shape
    grid = mesh.devices.reshape(sections, experts // (COLUMNS * CORES), COLUMNS, CORES)
    rows = ("z", "x", "core")
    return jax.shard_map(
        on_device,
        mesh=Mesh(grid, ("pipe",) + rows),
        in_specs=(
            P("pipe", rows, None),
            P("pipe", rows, None),
            P("pipe", rows, None),
            P("pipe", rows, None, None),
            P("pipe", rows, None, None),
        ),
        out_specs=(P("pipe", rows, None, None), P("pipe", rows, None)),
        check_vma=False,
    )
```

```python
from functools import partial

import jax
import jax.numpy as jnp
from jax import lax
from jax.experimental import pallas as pl
from jax.experimental.pallas import tpu as pltpu
from jax.sharding import Mesh, PartitionSpec as P

SCALE_ROUTED = 2.5
CORES = 2
WIDTH = 512
COSTS = 3.0, 3.0, 14.0, 8.0
COLUMNS = 4
LANES = 128
SMALL_VMEM = 12 * 2**20
PROJECT_VMEM = 57 * 2**20
LAST_VMEM = 48 * 2**20


def iota(shape, dim):
    return lax.broadcasted_iota(jnp.int32, shape, dim)


def call(body, out_shape, cost, vmem=SMALL_VMEM, **kwargs):
    return pl.pallas_call(
        body,
        out_shape=out_shape,
        cost_estimate=pl.CostEstimate(flops=cost[0], bytes_accessed=cost[1], transcendentals=0),
        compiler_params=pltpu.CompilerParams(vmem_limit_bytes=vmem),
        **kwargs,
    )


def ranks_before(hits):
    tokens = hits.shape[1]
    first, second = iota((tokens, tokens), 0), iota((tokens, tokens), 1)
    ahead = (first < second) & (first // LANES == second // LANES)
    ahead = jnp.where(ahead, 1.0, 0.0).astype(jnp.bfloat16)
    return jnp.dot(hits.astype(jnp.bfloat16), ahead, preferred_element_type=jnp.float32)


def gate_rows(affinity):
    total = jnp.sum(affinity, axis=0, keepdims=True)
    weights = (SCALE_ROUTED * affinity / total).astype(jnp.bfloat16).astype(jnp.float32)
    return total, weights


def matches(group_ref, z, experts, each):
    top, tokens = group_ref.shape[0] // 2, group_ref.shape[1]
    _, weights = gate_rows(group_ref[top:])
    labels = (z * experts + iota((16, tokens), 0)).astype(jnp.float32)
    hits = jnp.zeros((16, tokens), jnp.float32)
    gains = jnp.zeros((16, tokens), jnp.float32)
    for k in range(top):
        named = group_ref[k : k + 1, :] == labels
        hits += jnp.where(named, 1.0, 0.0)
        gains += jnp.where(named, weights[k : k + 1, :], 0.0)
    slot = ranks_before(hits).astype(jnp.int32) + (iota((16, tokens), 1) // LANES) * (each // CORES)
    slot = jnp.where(hits > 0, slot, -1)
    order = iota((each, tokens), 0)
    lines, columns = [], []
    for at in range(experts):
        s = (at % COLUMNS) * CORES + at // COLUMNS
        found = order == slot[s : s + 1, :]
        lines.append(jnp.where(found, 1.0, 0.0))
        columns.append(jnp.sum(jnp.where(found, gains[s : s + 1, :], 0.0), axis=1, keepdims=True))
    return jnp.concatenate(lines, axis=0).astype(jnp.bfloat16), jnp.concatenate(columns, axis=0)


def select_kernel(parts, capacity, place_ref, token_ref, *refs):
    groups = refs[: max(parts) + 1]
    blocks = refs[len(groups) : len(groups) + len(parts)]
    out_hbm, token_out, gain_ref, out_ref, out_sems = refs[-5:]
    count, rows, width = out_ref.shape
    tile = width // 2
    each = CORES * capacity
    token_out[...] = token_ref[...]
    found = [matches(group_ref, place_ref[0], rows // each, each) for group_ref in groups]
    stores = []
    for j in range(count):
        half = j if count == 1 or j == 2 else jnp.bitwise_xor(j, place_ref[1])
        for h in range(2):
            lanes = slice(h * tile, (h + 1) * tile)
            picked = jnp.dot(found[parts[j]][0], blocks[j][:, lanes], preferred_element_type=jnp.float32)
            out_ref[j, :, lanes] = picked.astype(jnp.bfloat16)
            at = pl.multiple_of(half * width + h * tile, LANES)
            store = pltpu.make_async_copy(
                out_ref.at[j, :, lanes], out_hbm.at[:, pl.ds(at, tile)], out_sems.at[2 * j + h]
            )
            store.start()
            stores.append(store)
    lane = iota((rows, LANES), 1)
    table = jnp.zeros((rows, LANES), jnp.float32)
    for i, (_, column) in enumerate(found):
        table = jnp.where(lane == i, column, table)
    gain_ref[...] = table.astype(jnp.bfloat16)
    store = pltpu.make_async_copy(gain_ref, out_hbm.at[:, count * width :], out_sems.at[2 * count])
    store.start()
    for store in stores + [store]:
        store.wait()


def select_rows(place, token, groups, blocks, parts, rows, capacity, micros):
    tokens, width = blocks[0].shape
    count = len(blocks)
    outside = pl.BlockSpec(memory_space=pltpu.HBM)
    inside = pl.BlockSpec(memory_space=pltpu.VMEM)
    return call(
        partial(select_kernel, parts, capacity),
        (
            jax.ShapeDtypeStruct((rows, width * count + LANES), jnp.bfloat16),
            jax.ShapeDtypeStruct(token.shape, token.dtype),
        ),
        (int(micros * 1.1e9), 2 * (rows + tokens) * width * count),
        grid_spec=pltpu.PrefetchScalarGridSpec(
            num_scalar_prefetch=1,
            in_specs=[inside] * (1 + len(groups) + count),
            out_specs=(outside, inside),
            scratch_shapes=[
                pltpu.VMEM((rows, LANES), jnp.bfloat16),
                pltpu.VMEM((count, rows, width), jnp.bfloat16),
                pltpu.SemaphoreType.DMA((2 * count + 1,)),
            ],
        ),
    )(place, token, *groups, *blocks)


def project_kernel(full, half, capacity, zs_ref, x_ref, w_ref, *refs):
    count = CORES * full + half
    saved, scores_in = refs[:count], refs[count]
    hidden_hbm, scores_ref, y_ref, out_ref, total_ref, out_sems = refs[-6:]
    n, chunks = pl.program_id(0), out_ref.shape[0]
    slots, width = out_ref.shape[2:]
    features = w_ref.shape[1]
    middle = features // 2
    at = features * full
    gain_at = at + middle * half
    dims = (((1,), (1,)), ((), ()))

    def times(x, w):
        return lax.dot_general(x, w, dims, preferred_element_type=jnp.float32)

    def store(step, j):
        lanes = pl.ds(pl.multiple_of(step * width, LANES), width)
        return pltpu.make_async_copy(
            out_ref.at[step, j], hidden_hbm.at[zs_ref[j], :, lanes], out_sems.at[step, j]
        )

    @pl.when(n == 0)
    def _():
        total_ref[...] = jnp.zeros(total_ref.shape, jnp.float32)
        scores_ref[...] = scores_in[...]

    if full:
        y_ref[: 2 * slots] = times(x_ref[:, :features], w_ref[...])
    if half:
        y_ref[2 * slots * full :] = times(x_ref[:slots, at : at + middle], w_ref[:, :middle]) + times(
            x_ref[slots:, at : at + middle], w_ref[:, middle:]
        )
    for j in range(count):
        whole = full and j < CORES
        top = j * slots if whole else 0
        lane = 0 if whole or not full else 1
        tile = x_ref[top : top + slots, gain_at : gain_at + LANES].astype(jnp.float32)
        gain = jnp.broadcast_to(tile[:, lane : lane + 1], (slots, LANES))
        total = total_ref[j]
        for i in range(0, width, LANES):
            lanes = slice(i, i + LANES)
            projected = y_ref[j * slots : (j + 1) * slots, lanes]
            out_ref[n, j, :, lanes] = (gain * projected).astype(jnp.bfloat16)
            total += projected * saved[j][0, :, lanes].astype(jnp.float32)
        total_ref[j] = total
        store(n, j).start()

    @pl.when(n == chunks - 1)
    def _():
        row = iota((slots, LANES), 0)
        own_lane = iota((slots, LANES), 1) == row % capacity
        sources = slots // capacity
        place = iota((sources, LANES), 0)
        for j in range(count):
            column = jnp.sum(total_ref[j], axis=1, keepdims=True)
            spread = jnp.where(own_lane, column, 0.0)
            table = jnp.zeros((sources, LANES), jnp.float32)
            for s in range(sources):
                line = jnp.sum(jnp.where(row // capacity == s, spread, 0.0), axis=0, keepdims=True)
                table = jnp.where(place == s, line, table)
            scores_ref[pl.ds(pl.multiple_of(zs_ref[j] * sources, sources), sources), :] = table
        for step in range(chunks):
            for j in range(count):
                store(step, j).wait()


def project(zs, rows, weight, saved, scores, hidden, full, half, capacity):
    count = CORES * full + half
    blocks, slots, units = saved.shape
    width = WIDTH
    chunks = units // width
    whole = lambda n, zs: (0, 0)
    inside = pl.BlockSpec(memory_space=pltpu.VMEM)
    outside = pl.BlockSpec(memory_space=pltpu.HBM)
    in_specs = [inside, pl.BlockSpec((width, weight.shape[1]), lambda n, zs: (n, 0))]
    in_specs += [pl.BlockSpec((1, slots, width), lambda n, zs, j=j: (zs[j], 0, n)) for j in range(count)]
    in_specs += [pl.BlockSpec(scores.shape, whole)]
    operands = [zs, rows, weight] + [saved] * count + [scores]
    aliases = {}
    if hidden is not None:
        in_specs.append(outside)
        aliases = {len(operands): 0}
        operands.append(hidden)
    return call(
        partial(project_kernel, full, half, capacity),
        (
            jax.ShapeDtypeStruct(saved.shape, jnp.bfloat16),
            jax.ShapeDtypeStruct(scores.shape, jnp.float32),
        ),
        (2 * rows.size * units, 2 * (rows.size + weight.size + 2 * count * slots * units)),
        vmem=LAST_VMEM if full and half else PROJECT_VMEM,
        grid_spec=pltpu.PrefetchScalarGridSpec(
            num_scalar_prefetch=1,
            grid=(chunks,),
            in_specs=in_specs,
            out_specs=(outside, pl.BlockSpec(scores.shape, whole)),
            scratch_shapes=[
                pltpu.VMEM((count * slots, width), jnp.float32),
                pltpu.VMEM((chunks, count, slots, width), jnp.bfloat16),
                pltpu.VMEM((count, slots, LANES), jnp.float32),
                pltpu.SemaphoreType.DMA((chunks, count)),
            ],
        ),
        input_output_aliases=aliases,
    )(*operands)


def gate_kernel(capacity, scores_ref, routes_ref, affinity_ref, out_ref):
    top = routes_ref.shape[0]
    total, weights = gate_rows(affinity_ref[...])
    labels = iota(scores_ref.shape, 0)
    hits = jnp.zeros(labels.shape, jnp.float32)
    for k in range(top):
        hits += jnp.where(routes_ref[k : k + 1, :] == labels, 1.0, 0.0)
    slot = jnp.where(hits > 0, ranks_before(hits), -1.0).astype(jnp.int32)
    found = jnp.zeros(labels.shape, jnp.float32)
    for r in range(capacity):
        found = jnp.where(slot == r, scores_ref[:, r : r + 1], found)
    place = iota((top, LANES), 0)
    grad = jnp.zeros((top, LANES), jnp.float32)
    for k in range(top):
        line = jnp.sum(jnp.where(routes_ref[k : k + 1, :] == labels, found, 0.0), axis=0, keepdims=True)
        grad = jnp.where(place == k, line, grad)
    weighted = jnp.sum(weights * grad, axis=0, keepdims=True)
    out_ref[...] = (SCALE_ROUTED / total) * grad - weighted / total


def on_device(upstream, routes, affinity, w_down, saved_hidden):
    sections, depth = lax.axis_size("pipe"), lax.axis_size("z")
    section, z, core = lax.axis_index("pipe"), lax.axis_index("z"), lax.axis_index("core")
    everyone = ("z", "x", "core")
    expert_count = depth * COLUMNS * CORES
    local = COLUMNS * CORES
    slot_total, units = saved_hidden.shape[2:]
    capacity = slot_total // expert_count
    tokens, features = upstream.shape[1:]
    half = features // 2
    cores = range(CORES)

    last = sections - 1
    near = lax.ppermute(upstream[0], "pipe", [(i, i - 1) for i in range(1, sections)])

    routes_own = routes[0].T
    affinity_own = affinity[0].T
    choices = jnp.concatenate([routes_own.astype(jnp.float32), affinity_own], 0)
    choices_mate = lax.ppermute(choices, "core", [(c, 1 - c) for c in cores])

    def in_order(a, b, axis):
        return jnp.where(core == 0, jnp.concatenate([a, b], axis), jnp.concatenate([b, a], axis))

    def along(block, distance, cross=False):
        pairs = []
        for i in range(depth):
            pairs.append((i * CORES + (1 if cross else 0), (i + distance) % depth * CORES))
            pairs.append((i * CORES + (0 if cross else 1), (i - distance) % depth * CORES + 1))
        return lax.ppermute(block, ("z", "core"), pairs)

    reach = depth // 2
    place = jnp.stack([z, core])
    rows = local * CORES * capacity
    choices = [in_order(choices, choices_mate, 1)]
    choices += [along(choices[0], k) for k in range(1, reach + 1)]
    token = jnp.zeros((8, LANES), jnp.float32)

    def exchange(block, axes, parts):
        shape = block.shape
        block = block.reshape(parts, shape[0] // parts, shape[1])
        return lax.all_to_all(block, axes, split_axis=0, concat_axis=0, tiled=True).reshape(shape)

    near, choices = lax.optimization_barrier((near, choices))
    incoming = jnp.where(section == last, upstream[0], near)
    mine = lax.dynamic_slice(incoming, (0, core * half), (tokens, half))
    other = lax.dynamic_slice(incoming, (0, (1 - core) * half), (tokens, half))
    mate = lax.ppermute(other, "core", [(c, 1 - c) for c in cores])
    held = in_order(mine, mate, 0)
    weight = w_down[0, 0]
    saved = saved_hidden[0, 0].reshape(depth, slot_total // depth, units)
    scores = jnp.zeros((expert_count, LANES), jnp.float32)

    def at(*distances):
        return jnp.stack([(z + d) % depth for d in distances])

    def columns(groups, blocks, parts, micros):
        picked, after = select_rows(place, token, groups, blocks, parts, rows, capacity, micros)
        return exchange(picked, ("core", "x"), local), after

    groups = []
    same, cross = along(held, 1), along(held, 1, cross=True)
    got, token = columns(choices[:1], [held], (0,), COSTS[0])
    groups.append((got, at(0), 0, 1))
    for k in range(1, reach - 1):
        same, cross, token = lax.optimization_barrier((same, cross, token))
        ahead = along(same, 1), along(cross, 1)
        got, token = columns([choices[k]], [same, cross], (0, 0), COSTS[k])
        groups.append((got, at(-k, k), 1, 0))
        same, cross = ahead
    k = reach - 1
    same, cross, token = lax.optimization_barrier((same, cross, token))
    got, token = columns(choices[k:], [same, cross, along(same, 1)], (0, 0, 1), COSTS[k])
    groups.append((got, at(-k, k, reach), 1, 1))

    hidden = None
    for got, zs, full, part in groups:
        hidden, scores = project(zs, got, weight, saved, scores, hidden, full, part, capacity)

    returned = exchange(scores, everyone, expert_count)
    affinity_grad = call(
        partial(gate_kernel, capacity),
        jax.ShapeDtypeStruct(affinity_own.shape, jnp.float32),
        (10**6, 10**5),
    )(returned, routes_own, affinity_own)
    return hidden.reshape(1, 1, slot_total, units), affinity_grad.T[None]


def solution(mesh):
    sections, experts = mesh.devices.shape
    grid = mesh.devices.reshape(sections, experts // (COLUMNS * CORES), COLUMNS, CORES)
    rows = ("z", "x", "core")
    return jax.shard_map(
        on_device,
        mesh=Mesh(grid, ("pipe",) + rows),
        in_specs=(
            P("pipe", rows, None),
            P("pipe", rows, None),
            P("pipe", rows, None),
            P("pipe", rows, None, None),
            P("pipe", rows, None, None),
        ),
        out_specs=(P("pipe", rows, None, None), P("pipe", rows, None)),
        check_vma=False,
    )
```
